256 devices in a mesh: ctx: 16 (over y, x), grp: 16 (over z, core).
Axes of the slice: x: 4, y: 4, z: 8, core: 2. Of those that a mesh axis runs over, the one named last changes fastest.
Arguments:
- q_in: bfloat16 [2048, 8192], P('ctx', 'grp'), may hold values from -170 to 170
- k_in: bfloat16 [2048, 8192], P('ctx', 'grp'), may hold values from -6 to 6
- v_in: bfloat16 [2048, 8192], P('ctx', 'grp'), may hold values from -6 to 6
- fir: float32 [3, 3, 8192], P(None, None, 'grp'), may hold values from -3 to 3
- skip: float32 [8192], P('grp'), may hold values from 0.2 to 1
- taps: bfloat16 [64, 2048], P('grp'), may hold values from -0.25 to 0.25
- segments: int32 [2048], P('ctx'), may hold values from 0 to 1, never falling along the last dimension, each value on 1 to 1920 neighbouring positions
- gain: float32 [8192], P('grp'), may hold values from 0.1 to 1.9
Outputs:
- mixed: bfloat16 [2048, 8192], P('ctx', 'grp')
The draws below stay inside these ranges and needn't reach their ends.
All inputs are finite; a program needn't handle non-finite values.
Results may differ from the reference program's by a relative error of at most 0.0085.
Values may be sent and summed in bfloat16 or wider, within the bound.
No kernel may reach another device: no remote copies, remote signals or barrier semaphores. Data moves between devices by JAX's collectives and lax.ppermute only.
A program may use at most 64 MiB of HBM per device.

```python
import math
import jax
import jax.numpy as jnp
import numpy as np
from jax import lax

D = 8192
GW = 128
TOK_DEV = 128
TOKENS = 2048
FG = 64
SEGS = 2
LONGEST = 1920


def draw_q_in(key, part):
    key_base = jax.random.fold_in(key, 11)
    key_cols = jax.random.fold_in(key, 12)
    key_rows = jax.random.fold_in(key, 13)
    base = jax.random.truncated_normal(key_base, -4.0, 4.0, (TOKENS, D), jnp.float32)
    rise = 3.0
    top = 4.0
    columns = jnp.exp(jax.random.uniform(key_cols, (D,), jnp.float32, 0.0, math.log(top)))
    columns = columns * rise ** (jnp.arange(D, dtype=jnp.float32) / D)
    rows_scale = jnp.exp(jax.random.uniform(key_rows, (TOKENS, 1), jnp.float32, 0.0, math.log(3.5)))
    return (base * rows_scale * columns).astype(jnp.bfloat16)


def block_scale(stream_key, dims, pieces, smallest, largest):
    def one(axis_at, blocks):
        draws = jax.random.uniform(jax.random.fold_in(jax.random.fold_in(stream_key, 6), axis_at), (blocks,), jnp.float32, smallest / len(pieces), largest / len(pieces))
        return jnp.repeat(jnp.exp(draws), dims[axis_at] // blocks).reshape((-1,) + (1,) * (len(dims) - axis_at - 1))

    level = one(*pieces[0])
    for cut in pieces[1:]:
        level = level * one(*cut)
    return level


def split_up(count, total, limit, slope):
    weights = [(1 << 20) // math.isqrt(grade ** slope) + 1 for grade in range(2, count + 1)]
    rest, counts = total - limit - (count - 1), [1] * (count - 1)
    while rest > 0:
        free = [i for i in range(count - 1) if counts[i] < limit]
        mass, left = sum([weights[i] for i in free]), rest
        for i in free:
            addition = min(limit - counts[i], max(1, left * weights[i] // mass), rest)
            counts[i] = counts[i] + addition
            rest = rest - addition
    return np.array([limit] + counts)


def uneven(stream_key, number_of, total, reach, skew):
    if number_of == 2:
        one = jax.random.randint(stream_key, (), max(1, total - reach), min(reach, total - 1) + 1)
        return jnp.stack([one, total - one])
    lengths = jnp.asarray(split_up(number_of, total, reach, skew), jnp.int32)
    pairs = (number_of - 1) // 2
    source_of, sink = lengths[1:1 + 2 * pairs:2], lengths[2:2 + 2 * pairs:2]
    room = jnp.minimum(source_of - 1, reach - sink)
    passed = jax.random.randint(jax.random.fold_in(stream_key, 1), (pairs,), 0, 1 << 20) % (room + 1)
    lengths = lengths.at[1:1 + 2 * pairs:2].set(source_of - passed).at[2:2 + 2 * pairs:2].set(sink + passed)
    return lengths[jax.random.permutation(jax.random.fold_in(stream_key, 2), number_of)]


def scatter_about(own_key, dims, deviation, limit, shards=(), kind=jnp.bfloat16):
    factor_of = block_scale(own_key, dims, shards, -0.22, 0.18) if shards else 1.0
    result = jax.random.normal(own_key, dims, jnp.float32) * deviation * factor_of
    return jnp.minimum(jnp.maximum(result, -limit), limit).astype(kind)


def setup_inputs(seed: int = 0) -> dict:
    keys = jax.random.split(jax.random.key(seed), 9)
    q_in = draw_q_in(jax.random.fold_in(keys[8], 71), 0)
    k_in = scatter_about(keys[1], (TOKENS, D), 1.0, 6.0, ((0, 16), (1, 16)))
    v_in = scatter_about(keys[2], (TOKENS, D), 1.0, 6.0, ((0, 16), (1, 16)))
    fir = scatter_about(keys[3], (3, 3, D), 0.6, 3.0, ((2, 16),), jnp.float32)
    skip = jnp.clip(jnp.exp(math.log(1.0) - 1.609438 * jax.random.uniform(keys[4], (D,), jnp.float32) ** block_scale(keys[4], (D,), ((0, 16),), -0.2, 0.2)), 0.2, 1.0)
    taps = scatter_about(keys[5], (FG, TOKENS), (TOKENS // 4) ** -0.5, 0.25, ((0, 16),))
    segments = jnp.searchsorted(jnp.cumsum(uneven(keys[6], SEGS, TOKENS, LONGEST, 2)), jnp.arange(TOKENS), side="right").astype(jnp.int32)
    gain = jnp.clip(1.0 + 0.18 * jax.random.normal(keys[7], (D,), jnp.float32), 0.1, 1.9)
    return dict(q_in=q_in, k_in=k_in, v_in=v_in, fir=fir, skip=skip, taps=taps, segments=segments, gain=gain)


def toeplitz(taps_row, row_pos, row_seg, col_pos, col_seg):
    offsets = row_pos[:, None] - col_pos[None, :]
    allowed = (offsets >= 0) & (row_seg[:, None] == col_seg[None, :])
    entries = jnp.take(taps_row, jnp.clip(offsets, 0, taps_row.shape[0] - 1).astype(jnp.int32))
    return jnp.where(allowed, entries, jnp.zeros((), taps_row.dtype))

def reference(q_in, k_in, v_in, fir, skip, taps, segments, gain):
    stacked = jnp.stack([q_in, k_in, v_in]).astype(jnp.float32)
    padded = jnp.pad(stacked, ((0, 0), (2, 0), (0, 0)))
    filtered = fir[:, 0, None, :] * padded[:, 2:] + fir[:, 1, None, :] * padded[:, 1:-1] + fir[:, 2, None, :] * padded[:, :-2]
    product_kv = (filtered[1] * filtered[2]).astype(jnp.bfloat16)
    nblock = TOKENS // TOK_DEV
    seg_blocks = segments.reshape(nblock, TOK_DEV)
    local_pos = jnp.arange(TOK_DEV, dtype=jnp.int32)
    kv_groups = product_kv.reshape(TOKENS, FG, GW).transpose(1, 0, 2)

    def one_group(pair):
        taps_row, kv_group = pair
        kv_blocks = kv_group.reshape(nblock, TOK_DEV, GW)

        def one_block(block):
            row_pos = (block * TOK_DEV + local_pos).astype(jnp.int32)
            row_seg = seg_blocks[block]

            def add_source(source, running):
                col_seg = seg_blocks[source]
                col_pos = (source * TOK_DEV + local_pos).astype(jnp.int32)

                def work(total):
                    matrix = toeplitz(taps_row, row_pos, row_seg, col_pos, col_seg)
                    return total + jnp.dot(matrix, kv_blocks[source], preferred_element_type=jnp.float32)
                return lax.cond(col_seg[-1] >= row_seg[0], work, lambda total: total, running)
            return lax.fori_loop(0, block + 1, add_source, jnp.zeros((TOK_DEV, GW), jnp.float32))
        return lax.map(one_block, jnp.arange(nblock, dtype=jnp.int32)).reshape(TOKENS, GW)
    conv = lax.map(one_group, (taps, kv_groups)).transpose(1, 0, 2).reshape(TOKENS, D)
    gated = filtered[0] * (conv + skip * product_kv.astype(jnp.float32))
    squares = lax.optimization_barrier(jnp.sum(gated * gated, axis=1, keepdims=True))
    mixed = gated * lax.rsqrt(squares / D + 1e-06) * gain
    return mixed.astype(jnp.bfloat16)
```

```python
import jax
import jax.numpy as jnp
from jax import lax
from jax.experimental import pallas as pl
from jax.experimental.pallas import tpu as pltpu
from jax.sharding import PartitionSpec as P

D = 8192
GW = 128
NB = 16
TB = 128
CH = 32
ROWS = 3 * CH + 16


def pack_kernel(q_ref, k_ref, v_ref, seg_ref, out_ref):
    for n, ref in enumerate((k_ref, v_ref, q_ref)):
        value = ref[...].astype(jnp.float32).T.astype(jnp.bfloat16)
        out_ref[:, n * CH : (n + 1) * CH, :] = value.reshape(NB, CH, TB)
    seg = seg_ref[...].astype(jnp.float32).astype(jnp.bfloat16)
    out_ref[:, 3 * CH :, :] = jnp.broadcast_to(seg.reshape(1, 1, TB), (NB, ROWS - 3 * CH, TB))


def conv_kernel(idx_ref, x_ref, fir_ref, skip_ref, taps_ref, out_ref, coef_ref):
    index = idx_ref[0]
    tile = pl.multiple_of((index // 4) * GW, GW)
    rows = [fir_ref[a, :, pl.ds(tile, GW)] for a in range(3)]
    rows.append(skip_ref[:, pl.ds(tile, GW)])
    rows.append(jnp.zeros((6, GW), jnp.float32))
    coef_ref[:, 0:16] = jnp.concatenate(rows, axis=0).T
    coef = coef_ref[pl.ds(pl.multiple_of((index % 4) * CH, CH), CH), :]
    weights = [jnp.broadcast_to(coef[:, n : n + 1], (CH, TB)) for n in range(10)]

    taps = taps_ref[...].astype(jnp.float32)
    pick = lax.broadcasted_iota(jnp.int32, taps.shape, 0) == index // 4
    row = jnp.sum(jnp.where(pick, taps, 0.0), axis=0, keepdims=True)
    row_at = lax.broadcasted_iota(jnp.int32, (TB, TB), 0)
    col_at = lax.broadcasted_iota(jnp.int32, (TB, TB), 1)
    upper = col_at >= row_at
    before = jnp.zeros((TB, TB), jnp.float32)
    band = [jnp.zeros((TB, TB), jnp.bfloat16)]
    for m in range(NB):
        rolled = pltpu.roll(
            jnp.broadcast_to(row[:, m * TB : (m + 1) * TB], (TB, TB)), 0, 1, stride=1, stride_axis=0
        )
        band.append(jnp.where(upper, rolled, before).astype(jnp.bfloat16))
        before = rolled

    lane = lax.broadcasted_iota(jnp.int32, (CH, TB), 1)

    def filtered(a, which):
        lo, w = which * CH, ((3, 4, 5), (6, 7, 8), (0, 1, 2))[which]
        here = x_ref[a, lo : lo + CH, :].astype(jnp.float32)
        past = x_ref[a - 1, lo : lo + CH, :].astype(jnp.float32) if a else jnp.zeros_like(here)
        one = jnp.where(lane >= 1, pltpu.roll(here, 1, 1), pltpu.roll(past, 1, 1))
        two = jnp.where(lane >= 2, pltpu.roll(here, 2, 1), pltpu.roll(past, 2, 1))
        return weights[w[0]] * here + weights[w[1]] * one + weights[w[2]] * two

    product, second = [], []
    for a in range(NB):
        value = (filtered(a, 0) * filtered(a, 1)).astype(jnp.bfloat16)
        product.append(value)
        mask = x_ref[a, 3 * CH : 3 * CH + 1, :]
        second.append(value * mask)
    pairs = NB // 2
    lhs = []
    for source in (product, second):
        for pair in range(pairs):
            lhs.append(jnp.concatenate([source[2 * pair], source[2 * pair + 1]], axis=1))
    total = [None] * (2 * pairs)
    for d in range(pairs):
        matrix = jnp.concatenate(
            [
                jnp.concatenate([band[2 * d + 1], band[2 * d + 2]], axis=1),
                jnp.concatenate([band[2 * d], band[2 * d + 1]], axis=1),
            ],
            axis=0,
        )
        used = lhs[: pairs - d] + lhs[pairs : 2 * pairs - d]
        result = jnp.dot(jnp.concatenate(used, axis=0), matrix, preferred_element_type=jnp.float32)
        for n in range(pairs - d):
            for half in range(2):
                piece = result[(half * (pairs - d) + n) * CH :][:CH]
                at = half * pairs + n + d
                total[at] = piece if total[at] is None else total[at] + piece
    for a in range(NB):
        side = slice((a % 2) * TB, (a % 2 + 1) * TB)
        mask = x_ref[a, 3 * CH : 3 * CH + 1, :].astype(jnp.float32)
        conv = jnp.where(mask > 0.5, total[pairs + a // 2][:, side], total[a // 2][:, side])
        gated = filtered(a, 2) * (conv + weights[9] * product[a].astype(jnp.float32))
        out_ref[a] = gated.astype(jnp.bfloat16)


def square_kernel(x_ref, out_ref):
    value = x_ref[...].astype(jnp.float32)
    out_ref[...] = jnp.broadcast_to(jnp.sum(value * value, axis=0, keepdims=True), (NB, 1, TB))


def finish_kernel(x_ref, part_ref, gain_ref, out_ref):
    squares = jnp.sum(part_ref[...], axis=0)
    scale = lax.rsqrt(squares / D + 1e-06)
    value = (x_ref[...].astype(jnp.float32) * scale).T
    out_ref[...] = (value * gain_ref[...]).astype(jnp.bfloat16)


def on_device(q_in, k_in, v_in, fir, skip, taps, segments, gain):
    width = q_in.shape[1]
    payload = pl.pallas_call(
        pack_kernel, out_shape=jax.ShapeDtypeStruct((NB, ROWS, TB), jnp.bfloat16), name="pack"
    )(q_in, k_in, v_in, segments.reshape(1, TB))
    payload = lax.all_to_all(payload, "ctx", 0, 0, tiled=True)
    index = lax.axis_index("ctx").reshape(1)
    gated = pl.pallas_call(
        conv_kernel,
        out_shape=jax.ShapeDtypeStruct((NB, CH, TB), jnp.bfloat16),
        in_specs=[pl.BlockSpec(memory_space=pltpu.SMEM)] + [pl.BlockSpec(memory_space=pltpu.VMEM)] * 4,
        scratch_shapes=[pltpu.VMEM((GW, GW), jnp.float32)],
        name="conv",
    )(index, payload, fir, skip.reshape(1, width), taps)
    gated = lax.all_to_all(gated, "ctx", 0, 0, tiled=True).reshape(width, TB)
    part = pl.pallas_call(
        square_kernel, out_shape=jax.ShapeDtypeStruct((NB, 1, TB), jnp.float32), name="squares"
    )(gated)
    part = lax.all_to_all(part, "grp", 0, 0, tiled=True)
    return pl.pallas_call(
        finish_kernel, out_shape=jax.ShapeDtypeStruct((TB, width), jnp.bfloat16), name="finish"
    )(gated, part, gain.reshape(1, width))


def solution(mesh):
    return jax.shard_map(
        on_device,
        mesh=mesh,
        in_specs=(
            P("ctx", "grp"),
            P("ctx", "grp"),
            P("ctx", "grp"),
            P(None, None, "grp"),
            P("grp"),
            P("grp", None),
            P("ctx"),
            P("grp"),
        ),
        out_specs=P("ctx", "grp"),
        check_vma=False,
    )
```

```python
import jax
import jax.numpy as jnp
from jax import lax
from jax.experimental import pallas as pl
from jax.experimental.pallas import tpu as pltpu
from jax.sharding import PartitionSpec as P

D = 8192
GW = 128
NB = 16
TB = 128
CH = 32
HALO = 2 * CH
SEG = HALO + 8
ROWS = HALO + 16
F32 = jnp.float32
BF16 = jnp.bfloat16


def pack_kernel(k_ref, v_ref, q_ref, seg_ref, out_ref):
    for n, ref in enumerate((k_ref, v_ref)):
        value = ref[...].astype(F32).T.astype(BF16)
        out_ref[:, n * CH : (n + 1) * CH, :] = value.reshape(NB, CH, TB)
    tail = q_ref[TB - 16 :, :].astype(F32)[14:16]
    pieces = [tail[:, n * TB : (n + 1) * TB] for n in range(4)]
    pieces.append(jnp.broadcast_to(seg_ref[...].astype(F32), (8, TB)))
    extra = jnp.concatenate(pieces, axis=0).astype(BF16)
    out_ref[:, HALO:, :] = jnp.broadcast_to(extra.reshape(1, ROWS - HALO, TB), (NB, ROWS - HALO, TB))


def band_kernel(idx_ref, fir_ref, skip_ref, taps_ref, band_ref, weight_ref, coef_ref):
    index = idx_ref[0]
    tile = pl.multiple_of((index // 4) * GW, GW)
    rows = [fir_ref[a, :, pl.ds(tile, GW)] for a in (1, 2)]
    rows.append(skip_ref[:, pl.ds(tile, GW)])
    rows.append(jnp.zeros((1, GW), F32))
    coef_ref[:, 0:8] = jnp.concatenate(rows, axis=0).T
    coef = coef_ref[pl.ds(pl.multiple_of((index % 4) * CH, CH), CH), :]
    for n in range(7):
        weight_ref[n] = jnp.broadcast_to(coef[:, n : n + 1], (CH, TB))

    taps = taps_ref[...].astype(F32)
    pick = lax.broadcasted_iota(jnp.int32, taps.shape, 0) == index // 4
    row = jnp.sum(jnp.where(pick, taps, 0.0), axis=0, keepdims=True)
    row_at = lax.broadcasted_iota(jnp.int32, (TB, TB), 0)
    col_at = lax.broadcasted_iota(jnp.int32, (TB, TB), 1)
    upper = col_at >= row_at
    before = jnp.zeros((TB, TB), F32)
    band_ref[0] = before.astype(BF16)
    for m in range(NB):
        piece = jnp.broadcast_to(row[:, m * TB : (m + 1) * TB], (TB, TB))
        rolled = pltpu.roll(piece, 0, 1, stride=1, stride_axis=0)
        band_ref[m + 1] = jnp.where(upper, rolled, before).astype(BF16)
        before = rolled


def conv_kernel(x_ref, band_ref, weight_ref, out_ref):
    lane = lax.broadcasted_iota(jnp.int32, (CH, TB), 1)
    weights = [weight_ref[n] for n in range(7)]

    def filtered(a, which):
        lo = which * CH
        here = x_ref[a, lo : lo + CH, :].astype(F32)
        past = x_ref[a - 1, lo : lo + CH, :].astype(F32) if a else jnp.zeros_like(here)
        one = jnp.where(lane >= 1, pltpu.roll(here, 1, 1), pltpu.roll(past, 1, 1))
        two = jnp.where(lane >= 2, pltpu.roll(here, 2, 1), pltpu.roll(past, 2, 1))
        return weights[3 * which] * here + weights[3 * which + 1] * one + weights[3 * which + 2] * two

    product, second = [], []
    for a in range(NB):
        value = (filtered(a, 0) * filtered(a, 1)).astype(BF16)
        product.append(value)
        mask = x_ref[a, SEG : SEG + 1, :]
        second.append(value * mask)
    pairs = NB // 2
    lhs = []
    for source in (product, second):
        for pair in range(pairs):
            lhs.append(jnp.concatenate([source[2 * pair], source[2 * pair + 1]], axis=1))
    total = [None] * (2 * pairs)
    for d in range(pairs):
        matrix = jnp.concatenate(
            [
                jnp.concatenate([band_ref[2 * d + 1], band_ref[2 * d + 2]], axis=1),
                jnp.concatenate([band_ref[2 * d], band_ref[2 * d + 1]], axis=1),
            ],
            axis=0,
        )
        used = lhs[: pairs - d] + lhs[pairs : 2 * pairs - d]
        result = jnp.dot(jnp.concatenate(used, axis=0), matrix, preferred_element_type=F32)
        for n in range(pairs - d):
            for half in range(2):
                piece = result[(half * (pairs - d) + n) * CH :][:CH]
                at = half * pairs + n + d
                total[at] = piece if total[at] is None else total[at] + piece
    for a in range(NB):
        side = slice((a % 2) * TB, (a % 2 + 1) * TB)
        mask = x_ref[a, SEG : SEG + 1, :].astype(F32)
        conv = jnp.where(mask > 0.5, total[pairs + a // 2][:, side], total[a // 2][:, side])
        out_ref[a] = (conv + weights[6] * product[a].astype(F32)).astype(BF16)


def gate_kernel(idx_ref, q_ref, x_ref, fir_ref, out_ref):
    index = idx_ref[0]
    halo = x_ref[jnp.maximum(index - 1, 0)].astype(F32)[HALO : HALO + 8]
    halo = jnp.where(index > 0, halo, 0.0)
    row_at = lax.broadcasted_iota(jnp.int32, (TB, TB), 0)
    for n in range(4):
        lanes = slice(n * TB, (n + 1) * TB)
        here = q_ref[:, lanes].astype(F32)
        last, older = halo[2 * n + 1 : 2 * n + 2], halo[2 * n : 2 * n + 1]
        one = jnp.where(row_at == 0, last, pltpu.roll(here, 1, 0))
        two = jnp.where(row_at == 0, older, jnp.where(row_at == 1, last, pltpu.roll(here, 2, 0)))
        value = fir_ref[0, 0:1, lanes] * here + fir_ref[0, 1:2, lanes] * one + fir_ref[0, 2:3, lanes] * two
        out_ref[lanes, :] = value.T


def square_kernel(u_ref, gate_ref, out_ref):
    value = u_ref[...].astype(F32) * gate_ref[...]
    out_ref[...] = jnp.broadcast_to(jnp.sum(value * value, axis=0, keepdims=True), (NB, 1, TB))


def turn_kernel(u_ref, gate_ref, out_ref):
    for n in range(4):
        lanes = slice(n * TB, (n + 1) * TB)
        value = u_ref[lanes, :].astype(F32) * gate_ref[lanes, :]
        out_ref[:, lanes] = value.T


def finish_kernel(x_ref, part_ref, gain_ref, out_ref):
    squares = jnp.sum(part_ref[...], axis=0)
    scale = lax.rsqrt(squares / D + 1e-06)
    scale = jnp.broadcast_to(scale, (TB, TB)).T
    for n in range(4):
        lanes = slice(n * TB, (n + 1) * TB)
        out_ref[:, lanes] = (x_ref[:, lanes] * scale * gain_ref[:, lanes]).astype(BF16)


VM = pl.BlockSpec(memory_space=pltpu.VMEM)
SM = pl.BlockSpec(memory_space=pltpu.SMEM)


def keep(value):
    return pltpu.with_memory_space_constraint(value, pltpu.VMEM)


def on_device(q_in, k_in, v_in, fir, skip, taps, segments, gain):
    width = q_in.shape[1]
    index = lax.axis_index("ctx").reshape(1)
    payload = pl.pallas_call(
        pack_kernel,
        out_shape=pltpu.VMEM((NB, ROWS, TB), BF16),
        in_specs=[VM, VM, VM, VM],
        out_specs=VM,
        name="pack",
    )(k_in, v_in, q_in, segments.reshape(1, TB))
    payload = lax.all_to_all(payload, "ctx", 0, 0, tiled=True)
    band, weight = pl.pallas_call(
        band_kernel,
        out_shape=(pltpu.VMEM((NB + 1, TB, TB), BF16), pltpu.VMEM((7, CH, TB), F32)),
        in_specs=[SM, VM, VM, VM],
        out_specs=(VM, VM),
        scratch_shapes=[pltpu.VMEM((GW, GW), F32)],
        name="band",
    )(index, fir, skip.reshape(1, width), taps)
    mixed = pl.pallas_call(
        conv_kernel,
        out_shape=pltpu.VMEM((NB, CH, TB), BF16),
        in_specs=[VM, VM, VM],
        out_specs=VM,
        name="conv",
    )(keep(payload), keep(band), keep(weight))
    mixed = lax.all_to_all(mixed, "ctx", 0, 0, tiled=True).reshape(width, TB)
    gate = pl.pallas_call(
        gate_kernel,
        out_shape=pltpu.VMEM((width, TB), F32),
        in_specs=[SM, VM, VM, VM],
        out_specs=VM,
        name="gate",
    )(index, q_in, keep(payload), fir)
    part = pl.pallas_call(
        square_kernel,
        out_shape=pltpu.VMEM((NB, 1, TB), F32),
        in_specs=[VM, VM],
        out_specs=VM,
        name="squares",
    )(keep(mixed), keep(gate))
    part = lax.all_to_all(part, "grp", 0, 0, tiled=True)
    turned = pl.pallas_call(
        turn_kernel,
        out_shape=pltpu.VMEM((TB, width), F32),
        in_specs=[VM, VM],
        out_specs=VM,
        name="turn",
    )(keep(mixed), keep(gate))
    return pl.pallas_call(
        finish_kernel,
        out_shape=jax.ShapeDtypeStruct((TB, width), BF16),
        in_specs=[VM, VM, VM],
        out_specs=VM,
        name="finish",
    )(keep(turned), keep(part), gain.reshape(1, width))


def solution(mesh):
    return jax.shard_map(
        on_device,
        mesh=mesh,
        in_specs=(
            P("ctx", "grp"),
            P("ctx", "grp"),
            P("ctx", "grp"),
            P(None, None, "grp"),
            P("grp"),
            P("grp", None),
            P("ctx"),
            P("grp"),
        ),
        out_specs=P("ctx", "grp"),
        check_vma=False,
    )
```

```python
import jax
import jax.numpy as jnp
from jax import lax
from jax.experimental import pallas as pl
from jax.experimental.pallas import tpu as pltpu
from jax.sharding import PartitionSpec as P

D = 8192
GW = 128
NB = 16
TB = 128
CH = 32
HALO = 2 * CH
SEG = HALO + 8
ROWS = HALO + 16
F32 = jnp.float32
BF16 = jnp.bfloat16


def pack_kernel(k_ref, v_ref, q_ref, seg_ref, out_ref):
    index = lax.axis_index("ctx")
    for n, ref in enumerate((k_ref, v_ref)):
        value = ref[...].astype(F32).T.astype(BF16)
        out_ref[:, n * CH : (n + 1) * CH, :] = value.reshape(NB, CH, TB)
    tail = q_ref[TB - 16 :, :].astype(F32)[14:16]
    tail = jnp.concatenate([tail[:, n * TB : (n + 1) * TB] for n in range(4)], axis=0)
    seg = jnp.broadcast_to(seg_ref[...].astype(F32), (8, TB))
    for n in range(NB):
        here = jnp.where(index == n - 1, tail, 0.0)
        out_ref[n, HALO:, :] = jnp.concatenate([here, seg], axis=0).astype(BF16)


def prepare_kernel(fir_ref, skip_ref, taps_ref, gain_ref, q_ref, band_ref, weight_ref, gate_ref, row_ref, coef_ref):
    index = lax.axis_index("ctx")
    tile = pl.multiple_of((index // 4) * GW, GW)
    rows = [fir_ref[a, :, pl.ds(tile, GW)] for a in (1, 2)]
    rows.append(skip_ref[:, pl.ds(tile, GW)])
    rows.append(jnp.zeros((1, GW), F32))
    coef_ref[:, 0:8] = jnp.concatenate(rows, axis=0).T
    coef = coef_ref[pl.ds(pl.multiple_of((index % 4) * CH, CH), CH), :]
    for n in range(7):
        weight_ref[n] = jnp.broadcast_to(coef[:, n : n + 1], (CH, TB))
    row_ref[0:3] = fir_ref[0]
    row_ref[3:4] = gain_ref[...]

    taps = taps_ref[...].astype(F32)
    pick = lax.broadcasted_iota(jnp.int32, taps.shape, 0) == index // 4
    row = jnp.sum(jnp.where(pick, taps, 0.0), axis=0, keepdims=True)
    row_at = lax.broadcasted_iota(jnp.int32, (TB, TB), 0)
    col_at = lax.broadcasted_iota(jnp.int32, (TB, TB), 1)
    upper = col_at >= row_at
    before = jnp.zeros((TB, TB), F32)
    band_ref[0] = before.astype(BF16)
    for m in range(NB):
        piece = jnp.broadcast_to(row[:, m * TB : (m + 1) * TB], (TB, TB))
        rolled = pltpu.roll(piece, 0, 1, stride=1, stride_axis=0)
        band_ref[m + 1] = jnp.where(upper, rolled, before).astype(BF16)
        before = rolled

    for n in range(4):
        lanes = slice(n * TB, (n + 1) * TB)
        here = q_ref[:, lanes].astype(F32)
        one = jnp.where(row_at == 0, 0.0, pltpu.roll(here, 1, 0))
        two = jnp.where(row_at <= 1, 0.0, pltpu.roll(here, 2, 0))
        value = fir_ref[0, 0:1, lanes] * here + fir_ref[0, 1:2, lanes] * one + fir_ref[0, 2:3, lanes] * two
        gate_ref[lanes, :] = value.T


def conv_kernel(x_ref, band_ref, weight_ref, out_ref):
    lane = lax.broadcasted_iota(jnp.int32, (CH, TB), 1)
    weights = [weight_ref[n] for n in range(7)]

    def filtered(a, which):
        lo = which * CH
        here = x_ref[a, lo : lo + CH, :].astype(F32)
        past = x_ref[a - 1, lo : lo + CH, :].astype(F32) if a else jnp.zeros_like(here)
        one = jnp.where(lane >= 1, pltpu.roll(here, 1, 1), pltpu.roll(past, 1, 1))
        two = jnp.where(lane >= 2, pltpu.roll(here, 2, 1), pltpu.roll(past, 2, 1))
        return weights[3 * which] * here + weights[3 * which + 1] * one + weights[3 * which + 2] * two

    product, second = [], []
    for a in range(NB):
        value = (filtered(a, 0) * filtered(a, 1)).astype(BF16)
        product.append(value)
        mask = x_ref[a, SEG : SEG + 1, :]
        second.append(value * mask)
    pairs = NB // 2
    lhs = []
    for source in (product, second):
        for pair in range(pairs):
            lhs.append(jnp.concatenate([source[2 * pair], source[2 * pair + 1]], axis=1))
    total = [None] * (2 * pairs)
    for d in range(pairs):
        matrix = jnp.concatenate(
            [
                jnp.concatenate([band_ref[2 * d + 1], band_ref[2 * d + 2]], axis=1),
                jnp.concatenate([band_ref[2 * d], band_ref[2 * d + 1]], axis=1),
            ],
            axis=0,
        )
        used = lhs[: pairs - d] + lhs[pairs : 2 * pairs - d]
        result = jnp.dot(jnp.concatenate(used, axis=0), matrix, preferred_element_type=F32)
        for n in range(pairs - d):
            for half in range(2):
                piece = result[(half * (pairs - d) + n) * CH :][:CH]
                at = half * pairs + n + d
                total[at] = piece if total[at] is None else total[at] + piece
    for a in range(NB):
        side = slice((a % 2) * TB, (a % 2 + 1) * TB)
        mask = x_ref[a, SEG : SEG + 1, :].astype(F32)
        conv = jnp.where(mask > 0.5, total[pairs + a // 2][:, side], total[a // 2][:, side])
        out_ref[a] = (conv + weights[6] * product[a].astype(F32)).astype(BF16)


def square_kernel(u_ref, gate_ref, x_ref, row_ref, part_ref, turned_ref):
    halo = x_ref[0, HALO:, :].astype(F32)
    for n in range(1, NB):
        halo = halo + x_ref[n, HALO:, :].astype(F32)
    row_at = lax.broadcasted_iota(jnp.int32, (TB, TB), 0)
    squares = jnp.zeros((1, TB), F32)
    for n in range(4):
        lanes = slice(n * TB, (n + 1) * TB)
        older, last = halo[2 * n : 2 * n + 1], halo[2 * n + 1 : 2 * n + 2]
        zero = row_ref[1:2, lanes] * last + row_ref[2:3, lanes] * older
        one = row_ref[2:3, lanes] * last
        extra = jnp.where(row_at == 0, zero, jnp.where(row_at == 1, one, 0.0)).T
        gated = u_ref[lanes, :].astype(F32) * (gate_ref[lanes, :] + extra)
        squares = squares + jnp.sum(gated * gated, axis=0, keepdims=True)
        turned_ref[:, lanes] = gated.T * row_ref[3:4, lanes]
    part_ref[...] = jnp.broadcast_to(squares, (NB, 1, TB))


def finish_kernel(x_ref, part_ref, out_ref):
    squares = jnp.sum(part_ref[...], axis=0)
    scale = lax.rsqrt(squares / D + 1e-06)
    scale = jnp.broadcast_to(scale, (TB, TB)).T
    for n in range(4):
        lanes = slice(n * TB, (n + 1) * TB)
        out_ref[:, lanes] = (x_ref[:, lanes] * scale).astype(BF16)


VM = pl.BlockSpec(memory_space=pltpu.VMEM)
SM = pl.BlockSpec(memory_space=pltpu.SMEM)


def keep(value):
    return pltpu.with_memory_space_constraint(value, pltpu.VMEM)


def on_device(q_in, k_in, v_in, fir, skip, taps, segments, gain):
    width = q_in.shape[1]
    payload = pl.pallas_call(
        pack_kernel,
        out_shape=jax.ShapeDtypeStruct((NB, ROWS, TB), BF16),
        in_specs=[VM] * 4,
        out_specs=VM,
        name="pack",
    )(k_in, v_in, q_in, segments.reshape(1, TB))
    payload = lax.all_to_all(payload, "ctx", 0, 0, tiled=True)
    band, weight, gate, rows = pl.pallas_call(
        prepare_kernel,
        out_shape=(
            pltpu.VMEM((NB + 1, TB, TB), BF16),
            pltpu.VMEM((7, CH, TB), F32),
            pltpu.VMEM((width, TB), F32),
            pltpu.VMEM((8, width), F32),
        ),
        in_specs=[VM] * 5,
        out_specs=(VM,) * 4,
        scratch_shapes=[pltpu.VMEM((GW, GW), F32)],
        name="prepare",
    )(fir, skip.reshape(1, width), taps, gain.reshape(1, width), q_in)
    mixed = pl.pallas_call(
        conv_kernel,
        out_shape=pltpu.VMEM((NB, CH, TB), BF16),
        in_specs=[VM] * 3,
        out_specs=VM,
        name="conv",
    )(keep(payload), keep(band), keep(weight))
    mixed = lax.all_to_all(mixed, "ctx", 0, 0, tiled=True).reshape(width, TB)
    part, turned = pl.pallas_call(
        square_kernel,
        out_shape=(pltpu.VMEM((NB, 1, TB), F32), pltpu.VMEM((TB, width), F32)),
        in_specs=[VM] * 4,
        out_specs=(VM,) * 2,
        name="squares",
    )(keep(mixed), keep(gate), keep(payload), keep(rows))
    part = lax.all_to_all(part, "grp", 0, 0, tiled=True)
    return pl.pallas_call(
        finish_kernel,
        out_shape=jax.ShapeDtypeStruct((TB, width), BF16),
        in_specs=[VM] * 2,
        out_specs=VM,
        name="finish",
    )(keep(turned), keep(part))


def solution(mesh):
    return jax.shard_map(
        on_device,
        mesh=mesh,
        in_specs=(
            P("ctx", "grp"),
            P("ctx", "grp"),
            P("ctx", "grp"),
            P(None, None, "grp"),
            P("grp"),
            P("grp", None),
            P("ctx"),
            P("grp"),
        ),
        out_specs=P("ctx", "grp"),
        check_vma=False,
    )
```

```python
import jax
import jax.numpy as jnp
from jax import lax
from jax.experimental import pallas as pl
from jax.experimental.pallas import tpu as pltpu
from jax.sharding import PartitionSpec as P

D = 8192
GW = 128
NB = 16
TB = 128
CH = 32
HALO = 2 * CH
SEG = HALO + 8
ROWS = HALO + 16
F32 = jnp.float32
BF16 = jnp.bfloat16


def prepare_kernel(
    k_ref, v_ref, q_ref, seg_ref, fir_ref, skip_ref, taps_ref, gain_ref,
    out_ref, band_ref, weight_ref, gate_ref, row_ref, coef_ref,
):
    index = lax.axis_index("ctx")
    for n, ref in enumerate((k_ref, v_ref)):
        value = ref[...].astype(F32).T.astype(BF16)
        out_ref[:, n * CH : (n + 1) * CH, :] = value.reshape(NB, CH, TB)
    tail = q_ref[TB - 16 :, :].astype(F32)[14:16]
    tail = jnp.concatenate([tail[:, n * TB : (n + 1) * TB] for n in range(4)], axis=0)
    seg = jnp.broadcast_to(seg_ref[...].astype(F32), (8, TB))
    for n in range(NB):
        here = jnp.where(index == n - 1, tail, 0.0)
        out_ref[n, HALO:, :] = jnp.concatenate([here, seg], axis=0).astype(BF16)

    tile = pl.multiple_of((index // 4) * GW, GW)
    rows = [fir_ref[a, :, pl.ds(tile, GW)] for a in (1, 2)]
    rows.append(skip_ref[:, pl.ds(tile, GW)])
    rows.append(jnp.zeros((1, GW), F32))
    coef_ref[:, 0:8] = jnp.concatenate(rows, axis=0).T
    coef = coef_ref[pl.ds(pl.multiple_of((index % 4) * CH, CH), CH), :]
    for n in range(7):
        weight_ref[n] = jnp.broadcast_to(coef[:, n : n + 1], (CH, TB))
    row_ref[0:3] = fir_ref[0]
    row_ref[3:4] = gain_ref[...]

    taps = taps_ref[...].astype(F32)
    pick = lax.broadcasted_iota(jnp.int32, taps.shape, 0) == index // 4
    row = jnp.sum(jnp.where(pick, taps, 0.0), axis=0, keepdims=True)
    row_at = lax.broadcasted_iota(jnp.int32, (TB, TB), 0)
    col_at = lax.broadcasted_iota(jnp.int32, (TB, TB), 1)
    upper = col_at >= row_at
    before = jnp.zeros((TB, TB), F32)
    band_ref[0] = before.astype(BF16)
    for m in range(NB):
        piece = jnp.broadcast_to(row[:, m * TB : (m + 1) * TB], (TB, TB))
        rolled = pltpu.roll(piece, 0, 1, stride=1, stride_axis=0)
        band_ref[m + 1] = jnp.where(upper, rolled, before).astype(BF16)
        before = rolled

    for n in range(4):
        lanes = slice(n * TB, (n + 1) * TB)
        here = q_ref[:, lanes].astype(F32)
        one = jnp.where(row_at == 0, 0.0, pltpu.roll(here, 1, 0))
        two = jnp.where(row_at <= 1, 0.0, pltpu.roll(here, 2, 0))
        value = fir_ref[0, 0:1, lanes] * here + fir_ref[0, 1:2, lanes] * one + fir_ref[0, 2:3, lanes] * two
        gate_ref[lanes, :] = value.T


def conv_kernel(x_ref, band_ref, weight_ref, out_ref):
    lane = lax.broadcasted_iota(jnp.int32, (CH, TB), 1)
    weights = [weight_ref[n] for n in range(7)]

    def filtered(a, which):
        lo = which * CH
        here = x_ref[a, lo : lo + CH, :].astype(F32)
        past = x_ref[a - 1, lo : lo + CH, :].astype(F32) if a else jnp.zeros_like(here)
        one = jnp.where(lane >= 1, pltpu.roll(here, 1, 1), pltpu.roll(past, 1, 1))
        two = jnp.where(lane >= 2, pltpu.roll(here, 2, 1), pltpu.roll(past, 2, 1))
        return weights[3 * which] * here + weights[3 * which + 1] * one + weights[3 * which + 2] * two

    product, second = [], []
    for a in range(NB):
        value = (filtered(a, 0) * filtered(a, 1)).astype(BF16)
        product.append(value)
        mask = x_ref[a, SEG : SEG + 1, :]
        second.append(value * mask)
    pairs = NB // 2
    lhs = []
    for source in (product, second):
        for pair in range(pairs):
            lhs.append(jnp.concatenate([source[2 * pair], source[2 * pair + 1]], axis=1))
    total = [None] * (2 * pairs)
    for d in range(pairs):
        matrix = jnp.concatenate(
            [
                jnp.concatenate([band_ref[2 * d + 1], band_ref[2 * d + 2]], axis=1),
                jnp.concatenate([band_ref[2 * d], band_ref[2 * d + 1]], axis=1),
            ],
            axis=0,
        )
        used = lhs[: pairs - d] + lhs[pairs : 2 * pairs - d]
        result = jnp.dot(jnp.concatenate(used, axis=0), matrix, preferred_element_type=F32)
        for n in range(pairs - d):
            for half in range(2):
                piece = result[(half * (pairs - d) + n) * CH :][:CH]
                at = half * pairs + n + d
                total[at] = piece if total[at] is None else total[at] + piece
    for a in range(NB):
        side = slice((a % 2) * TB, (a % 2 + 1) * TB)
        mask = x_ref[a, SEG : SEG + 1, :].astype(F32)
        conv = jnp.where(mask > 0.5, total[pairs + a // 2][:, side], total[a // 2][:, side])
        out_ref[a] = (conv + weights[6] * product[a].astype(F32)).astype(BF16)


def square_kernel(u_ref, gate_ref, x_ref, row_ref, part_ref, turned_ref):
    halo = x_ref[0, HALO:, :].astype(F32)
    for n in range(1, NB):
        halo = halo + x_ref[n, HALO:, :].astype(F32)
    row_at = lax.broadcasted_iota(jnp.int32, (TB, TB), 0)
    squares = jnp.zeros((1, TB), F32)
    for n in range(4):
        lanes = slice(n * TB, (n + 1) * TB)
        older, last = halo[2 * n : 2 * n + 1], halo[2 * n + 1 : 2 * n + 2]
        zero = row_ref[1:2, lanes] * last + row_ref[2:3, lanes] * older
        one = row_ref[2:3, lanes] * last
        extra = jnp.where(row_at == 0, zero, jnp.where(row_at == 1, one, 0.0)).T
        gated = u_ref[lanes, :].astype(F32) * (gate_ref[lanes, :] + extra)
        squares = squares + jnp.sum(gated * gated, axis=0, keepdims=True)
        turned_ref[:, lanes] = gated.T * row_ref[3:4, lanes]
    part_ref[...] = jnp.broadcast_to(squares, (NB, 1, TB))


def finish_kernel(x_ref, part_ref, out_ref):
    squares = jnp.sum(part_ref[...], axis=0)
    scale = lax.rsqrt(squares / D + 1e-06)
    scale = jnp.broadcast_to(scale, (TB, TB)).T
    for n in range(4):
        lanes = slice(n * TB, (n + 1) * TB)
        out_ref[:, lanes] = (x_ref[:, lanes] * scale).astype(BF16)


VM = pl.BlockSpec(memory_space=pltpu.VMEM)
SM = pl.BlockSpec(memory_space=pltpu.SMEM)


def keep(value):
    return pltpu.with_memory_space_constraint(value, pltpu.VMEM)


def on_device(q_in, k_in, v_in, fir, skip, taps, segments, gain):
    width = q_in.shape[1]
    payload, band, weight, gate, rows = pl.pallas_call(
        prepare_kernel,
        out_shape=(
            pltpu.VMEM((NB, ROWS, TB), BF16),
            pltpu.VMEM((NB + 1, TB, TB), BF16),
            pltpu.VMEM((7, CH, TB), F32),
            pltpu.VMEM((width, TB), F32),
            pltpu.VMEM((8, width), F32),
        ),
        in_specs=[VM] * 8,
        out_specs=(VM,) * 5,
        scratch_shapes=[pltpu.VMEM((GW, GW), F32)],
        name="prepare",
    )(
        k_in, v_in, q_in, segments.reshape(1, TB),
        fir, skip.reshape(1, width), taps, gain.reshape(1, width),
    )
    payload = lax.all_to_all(payload, "ctx", 0, 0, tiled=True)
    mixed = pl.pallas_call(
        conv_kernel,
        out_shape=pltpu.VMEM((NB, CH, TB), BF16),
        in_specs=[VM] * 3,
        out_specs=VM,
        name="conv",
    )(keep(payload), keep(band), keep(weight))
    mixed = lax.all_to_all(mixed, "ctx", 0, 0, tiled=True).reshape(width, TB)
    part, turned = pl.pallas_call(
        square_kernel,
        out_shape=(pltpu.VMEM((NB, 1, TB), F32), pltpu.VMEM((TB, width), F32)),
        in_specs=[VM] * 4,
        out_specs=(VM,) * 2,
        name="squares",
    )(keep(mixed), keep(gate), keep(payload), keep(rows))
    part = lax.all_to_all(part, "grp", 0, 0, tiled=True)
    return pl.pallas_call(
        finish_kernel,
        out_shape=jax.ShapeDtypeStruct((TB, width), BF16),
        in_specs=[VM] * 2,
        out_specs=VM,
        name="finish",
    )(keep(turned), keep(part))


def solution(mesh):
    return jax.shard_map(
        on_device,
        mesh=mesh,
        in_specs=(
            P("ctx", "grp"),
            P("ctx", "grp"),
            P("ctx", "grp"),
            P(None, None, "grp"),
            P("grp"),
            P("grp", None),
            P("ctx"),
            P("grp"),
        ),
        out_specs=P("ctx", "grp"),
        check_vma=False,
    )
```

```python
import jax
import jax.numpy as jnp
from jax import lax
from jax.experimental import pallas as pl
from jax.experimental.pallas import tpu as pltpu
from jax.sharding import PartitionSpec as P

D = 8192
GW = 128
NB = 16
TB = 128
CH = 32
HALO = CH
EDGE = HALO + 8
ROWS = HALO + 16
F32 = jnp.float32
BF16 = jnp.bfloat16


def one_hot(rows, by):
    row_at = lax.broadcasted_iota(jnp.int32, (rows, TB), 0)
    col_at = lax.broadcasted_iota(jnp.int32, (rows, TB), 1)
    return jnp.where(row_at == col_at + by, 1.0, 0.0).astype(BF16)


def fir_filter(ref, fir_ref, which, lanes, shifts):
    value = ref[:, lanes]
    moved = [jnp.dot(shift, value, preferred_element_type=F32) for shift in shifts]
    taps = [fir_ref[which, n : n + 1, lanes] for n in range(3)]
    return taps[0] * value.astype(F32) + taps[1] * moved[0] + taps[2] * moved[1]


def prepare_kernel(
    k_ref, v_ref, q_ref, seg_ref, fir_ref, skip_ref, taps_ref, gain_ref,
    out_ref, band_ref, weight_ref, gate_ref, row_ref, coef_ref,
):
    index = lax.axis_index("ctx")
    row_at = lax.broadcasted_iota(jnp.int32, (TB, TB), 0)
    col_at = lax.broadcasted_iota(jnp.int32, (TB, TB), 1)
    same, shifts = one_hot(TB, 0), (one_hot(TB, 1), one_hot(TB, 2))
    first = jnp.sum(jnp.where(seg_ref[...] == 0, 1.0, 0.0), axis=1, keepdims=True)
    tail = q_ref[TB - 16 :, :].astype(F32)[14:16]
    tail = jnp.concatenate([tail[:, n * TB : (n + 1) * TB] for n in range(4)], axis=0)
    heads = [ref[0:16, :].astype(F32)[0:2] for ref in (k_ref, v_ref)]
    tails = [ref[TB - 16 :, :].astype(F32)[14:16] for ref in (k_ref, v_ref)]
    edges = jnp.concatenate([heads[0], tails[0], heads[1], tails[1]], axis=0)
    for n in range(4):
        lanes = slice(n * TB, (n + 1) * TB)
        value = fir_filter(k_ref, fir_ref, 1, lanes, shifts) * fir_filter(v_ref, fir_ref, 2, lanes, shifts)
        value = lax.dot_general(
            same, value.astype(BF16), (((1,), (1,)), ((), ())), preferred_element_type=F32
        )
        value = jnp.where(col_at == 0, first, value)
        out_ref[4 * n : 4 * n + 4, 0:CH, :] = value.astype(BF16).reshape(4, CH, TB)
        gate_ref[lanes, :] = fir_filter(q_ref, fir_ref, 0, lanes, shifts).T
        for m in range(4):
            here = jnp.where(index == 4 * n + m - 1, tail, 0.0)
            edge = pltpu.roll(edges[:, lanes], (TB - m * CH) % TB, 1) if m else edges[:, lanes]
            out_ref[4 * n + m, HALO:, :] = jnp.concatenate([here, edge], axis=0).astype(BF16)

    tile = pl.multiple_of((index // 4) * GW, GW)
    rows = [fir_ref[a, :, pl.ds(tile, GW)] for a in (1, 2)]
    rows.append(skip_ref[:, pl.ds(tile, GW)])
    rows.append(jnp.zeros((1, GW), F32))
    coef_ref[:, 0:8] = jnp.concatenate(rows, axis=0).T
    coef = coef_ref[pl.ds(pl.multiple_of((index % 4) * CH, CH), CH), :]
    for n in range(7):
        weight_ref[n] = jnp.broadcast_to(coef[:, n : n + 1], (CH, TB))
    row_ref[0:3] = fir_ref[0]
    row_ref[3:4] = gain_ref[...]

    taps = taps_ref[...].astype(F32)
    pick = lax.broadcasted_iota(jnp.int32, taps.shape, 0) == index // 4
    row = jnp.sum(jnp.where(pick, taps, 0.0), axis=0, keepdims=True)
    upper = col_at >= row_at
    before = jnp.zeros((TB, TB), F32)
    band_ref[0] = before.astype(BF16)
    for m in range(NB):
        piece = jnp.broadcast_to(row[:, m * TB : (m + 1) * TB], (TB, TB))
        rolled = pltpu.roll(piece, 0, 1, stride=1, stride_axis=0)
        band_ref[m + 1] = jnp.where(upper, rolled, before).astype(BF16)
        before = rolled


def conv_kernel(x_ref, band_ref, weight_ref, out_ref):
    lane = lax.broadcasted_iota(jnp.int32, (CH, TB), 1)
    edges = jnp.concatenate([x_ref[a, HALO:, :].astype(F32)[8:16] for a in range(NB)], axis=0).T[0:CH]

    def ahead(by):
        return pltpu.roll(edges, TB - by, 1) if by else edges

    def behind(by):
        return jnp.where(lane < 8, 0.0, pltpu.roll(edges, by, 1))

    def pair(at, which):
        w = [weight_ref[3 * which + n] for n in range(3)]
        zero, one, older, last = ahead(at), ahead(at + 1), behind(6 - at), behind(5 - at)
        return w[0] * zero + w[1] * last + w[2] * older, w[0] * one + w[1] * zero + w[2] * last

    k_zero, k_one = pair(0, 0)
    v_zero, v_one = pair(4, 1)
    fixed = jnp.where(lane % 8 == 0, k_zero * v_zero, pltpu.roll(k_one * v_one, 1, 1))

    product, second, masks = [], [], []
    for a in range(NB):
        value = x_ref[a, 0:CH, :].astype(F32)
        mask = lane.astype(F32) >= jnp.broadcast_to(value[:, 0:1], (CH, TB))
        value = jnp.where(lane < 2, pltpu.roll(fixed, (TB - 8 * a) % TB, 1) if a else fixed, value)
        product.append(value.astype(BF16))
        second.append(jnp.where(mask, value, 0.0).astype(BF16))
        masks.append(mask)
    pairs = NB // 2
    lhs = []
    for source in (product, second):
        for at in range(pairs):
            lhs.append(jnp.concatenate([source[2 * at], source[2 * at + 1]], axis=1))
    total = [None] * (2 * pairs)
    for d in range(pairs):
        matrix = jnp.concatenate(
            [
                jnp.concatenate([band_ref[2 * d + 1], band_ref[2 * d + 2]], axis=1),
                jnp.concatenate([band_ref[2 * d], band_ref[2 * d + 1]], axis=1),
            ],
            axis=0,
        )
        used = lhs[: pairs - d] + lhs[pairs : 2 * pairs - d]
        result = jnp.dot(jnp.concatenate(used, axis=0), matrix, preferred_element_type=F32)
        for n in range(pairs - d):
            for half in range(2):
                piece = result[(half * (pairs - d) + n) * CH :][:CH]
                at = half * pairs + n + d
                total[at] = piece if total[at] is None else total[at] + piece
    for a in range(NB):
        side = slice((a % 2) * TB, (a % 2 + 1) * TB)
        conv = jnp.where(masks[a], total[pairs + a // 2][:, side], total[a // 2][:, side])
        out_ref[a] = (conv + weight_ref[6] * product[a].astype(F32)).astype(BF16)


def square_kernel(u_ref, gate_ref, x_ref, row_ref, part_ref, turned_ref):
    halo = x_ref[0, HALO:, :].astype(F32)
    for n in range(1, NB):
        halo = halo + x_ref[n, HALO:, :].astype(F32)
    row_at = lax.broadcasted_iota(jnp.int32, (TB, TB), 0)
    squares = jnp.zeros((1, TB), F32)
    for n in range(4):
        lanes = slice(n * TB, (n + 1) * TB)
        older, last = halo[2 * n : 2 * n + 1], halo[2 * n + 1 : 2 * n + 2]
        zero = row_ref[1:2, lanes] * last + row_ref[2:3, lanes] * older
        one = row_ref[2:3, lanes] * last
        extra = jnp.where(row_at == 0, zero, jnp.where(row_at == 1, one, 0.0)).T
        gated = u_ref[lanes, :].astype(F32) * (gate_ref[lanes, :] + extra)
        squares = squares + jnp.sum(gated * gated, axis=0, keepdims=True)
        turned_ref[:, lanes] = gated.T * row_ref[3:4, lanes]
    part_ref[...] = jnp.broadcast_to(squares, (NB, 1, TB))


def finish_kernel(x_ref, part_ref, out_ref):
    squares = jnp.sum(part_ref[...], axis=0)
    scale = lax.rsqrt(squares / D + 1e-06)
    scale = jnp.broadcast_to(scale, (TB, TB)).T
    for n in range(4):
        lanes = slice(n * TB, (n + 1) * TB)
        out_ref[:, lanes] = (x_ref[:, lanes] * scale).astype(BF16)


VM = pl.BlockSpec(memory_space=pltpu.VMEM)
SM = pl.BlockSpec(memory_space=pltpu.SMEM)


def keep(value):
    return pltpu.with_memory_space_constraint(value, pltpu.VMEM)


def on_device(q_in, k_in, v_in, fir, skip, taps, segments, gain):
    width = q_in.shape[1]
    payload, band, weight, gate, rows = pl.pallas_call(
        prepare_kernel,
        out_shape=(
            pltpu.VMEM((NB, ROWS, TB), BF16),
            pltpu.VMEM((NB + 1, TB, TB), BF16),
            pltpu.VMEM((7, CH, TB), F32),
            pltpu.VMEM((width, TB), F32),
            pltpu.VMEM((8, width), F32),
        ),
        in_specs=[VM] * 8,
        out_specs=(VM,) * 5,
        scratch_shapes=[pltpu.VMEM((GW, GW), F32)],
        name="prepare",
    )(
        k_in, v_in, q_in, segments.reshape(1, TB),
        fir, skip.reshape(1, width), taps, gain.reshape(1, width),
    )
    payload = lax.all_to_all(payload, "ctx", 0, 0, tiled=True)
    mixed = pl.pallas_call(
        conv_kernel,
        out_shape=pltpu.VMEM((NB, CH, TB), BF16),
        in_specs=[VM] * 3,
        out_specs=VM,
        name="conv",
    )(keep(payload), keep(band), keep(weight))
    mixed = lax.all_to_all(mixed, "ctx", 0, 0, tiled=True).reshape(width, TB)
    part, turned = pl.pallas_call(
        square_kernel,
        out_shape=(pltpu.VMEM((NB, 1, TB), F32), pltpu.VMEM((TB, width), F32)),
        in_specs=[VM] * 4,
        out_specs=(VM,) * 2,
        name="squares",
    )(keep(mixed), keep(gate), keep(payload), keep(rows))
    part = lax.all_to_all(part, "grp", 0, 0, tiled=True)
    return pl.pallas_call(
        finish_kernel,
        out_shape=jax.ShapeDtypeStruct((TB, width), BF16),
        in_specs=[VM] * 2,
        out_specs=VM,
        name="finish",
    )(keep(turned), keep(part))


def solution(mesh):
    return jax.shard_map(
        on_device,
        mesh=mesh,
        in_specs=(
            P("ctx", "grp"),
            P("ctx", "grp"),
            P("ctx", "grp"),
            P(None, None, "grp"),
            P("grp"),
            P("grp", None),
            P("ctx"),
            P("grp"),
        ),
        out_specs=P("ctx", "grp"),
        check_vma=False,
    )
```

```python
import jax
import jax.numpy as jnp
from jax import lax
from jax.experimental import pallas as pl
from jax.experimental.pallas import tpu as pltpu
from jax.sharding import PartitionSpec as P

D = 8192
GW = 128
NB = 16
TB = 128
CH = 32
HALO = CH
EDGE = HALO + 8
ROWS = HALO + 16
F32 = jnp.float32
BF16 = jnp.bfloat16


def fir_filter(ref, fir_ref, which, lanes, row_at=None):
    value = ref[:, lanes].astype(F32)
    one, two = pltpu.roll(value, 1, 0), pltpu.roll(value, 2, 0)
    if row_at is not None:
        one, two = jnp.where(row_at == 0, 0.0, one), jnp.where(row_at <= 1, 0.0, two)
    taps = [fir_ref[which, n : n + 1, lanes] for n in range(3)]
    return taps[0] * value + taps[1] * one + taps[2] * two


def prepare_kernel(
    k_ref, v_ref, q_ref, seg_ref, fir_ref, skip_ref, taps_ref, gain_ref,
    out_ref, band_ref, weight_ref, gate_ref, row_ref, coef_ref,
):
    index = lax.axis_index("ctx")
    row_at = lax.broadcasted_iota(jnp.int32, (TB, TB), 0)
    col_at = lax.broadcasted_iota(jnp.int32, (TB, TB), 1)
    same = jnp.where(row_at == col_at, 1.0, 0.0).astype(BF16)
    first = jnp.sum(jnp.where(seg_ref[...] == 0, 1.0, 0.0), axis=1, keepdims=True)
    tail = q_ref[TB - 16 :, :].astype(F32)[14:16]
    tail = jnp.concatenate([tail[:, n * TB : (n + 1) * TB] for n in range(4)], axis=0)
    heads = [ref[0:16, :].astype(F32)[0:2] for ref in (k_ref, v_ref)]
    tails = [ref[TB - 16 :, :].astype(F32)[14:16] for ref in (k_ref, v_ref)]
    edges = jnp.concatenate([heads[0], tails[0], heads[1], tails[1]], axis=0)
    for n in range(4):
        lanes = slice(n * TB, (n + 1) * TB)
        value = fir_filter(k_ref, fir_ref, 1, lanes) * fir_filter(v_ref, fir_ref, 2, lanes)
        value = lax.dot_general(
            same, value.astype(BF16), (((1,), (1,)), ((), ())), preferred_element_type=F32
        )
        value = jnp.where(col_at == 0, first, value)
        out_ref[4 * n : 4 * n + 4, 0:CH, :] = value.astype(BF16).reshape(4, CH, TB)
        gate_ref[lanes, :] = fir_filter(q_ref, fir_ref, 0, lanes, row_at).T
        for m in range(4):
            here = jnp.where(index == 4 * n + m - 1, tail, 0.0)
            edge = pltpu.roll(edges[:, lanes], (TB - m * CH) % TB, 1) if m else edges[:, lanes]
            out_ref[4 * n + m, HALO:, :] = jnp.concatenate([here, edge], axis=0).astype(BF16)

    tile = pl.multiple_of((index // 4) * GW, GW)
    rows = [fir_ref[a, :, pl.ds(tile, GW)] for a in (1, 2)]
    rows.append(skip_ref[:, pl.ds(tile, GW)])
    rows.append(jnp.zeros((1, GW), F32))
    coef_ref[:, 0:8] = jnp.concatenate(rows, axis=0).T
    coef = coef_ref[pl.ds(pl.multiple_of((index % 4) * CH, CH), CH), :]
    for n in range(7):
        weight_ref[n] = jnp.broadcast_to(coef[:, n : n + 1], (CH, TB))
    row_ref[0:3] = fir_ref[0]
    row_ref[3:4] = gain_ref[...]

    taps = taps_ref[...].astype(F32)
    pick = lax.broadcasted_iota(jnp.int32, taps.shape, 0) == index // 4
    row = jnp.sum(jnp.where(pick, taps, 0.0), axis=0, keepdims=True)
    upper = col_at >= row_at
    before = jnp.zeros((TB, TB), F32)
    band_ref[0] = before.astype(BF16)
    for m in range(NB):
        piece = jnp.broadcast_to(row[:, m * TB : (m + 1) * TB], (TB, TB))
        rolled = pltpu.roll(piece, 0, 1, stride=1, stride_axis=0)
        band_ref[m + 1] = jnp.where(upper, rolled, before).astype(BF16)
        before = rolled


def conv_kernel(x_ref, band_ref, weight_ref, out_ref):
    lane = lax.broadcasted_iota(jnp.int32, (CH, TB), 1)
    edges = jnp.concatenate([x_ref[a, HALO:, :].astype(F32)[8:16] for a in range(NB)], axis=0).T[0:CH]

    def ahead(by):
        return pltpu.roll(edges, TB - by, 1) if by else edges

    def behind(by):
        return jnp.where(lane < 8, 0.0, pltpu.roll(edges, by, 1))

    def pair(at, which):
        w = [weight_ref[3 * which + n] for n in range(3)]
        zero, one, older, last = ahead(at), ahead(at + 1), behind(6 - at), behind(5 - at)
        return w[0] * zero + w[1] * last + w[2] * older, w[0] * one + w[1] * zero + w[2] * last

    k_zero, k_one = pair(0, 0)
    v_zero, v_one = pair(4, 1)
    fixed = jnp.where(lane % 8 == 0, k_zero * v_zero, pltpu.roll(k_one * v_one, 1, 1))

    product, second, masks, after = [], [], [], []
    for a in range(NB):
        value = x_ref[a, 0:CH, :].astype(F32)
        first = jnp.broadcast_to(value[:, 0:1], (CH, TB))
        mask = lane.astype(F32) >= first
        if a % 2 == 0:
            after.append(jnp.concatenate([first, first], axis=1) == 0.0)
        value = jnp.where(lane < 2, pltpu.roll(fixed, (TB - 8 * a) % TB, 1) if a else fixed, value)
        product.append(value.astype(BF16))
        second.append(jnp.where(mask, value, 0.0).astype(BF16))
        masks.append(mask)
    pairs = NB // 2
    full = [jnp.concatenate(product[2 * at : 2 * at + 2], axis=1) for at in range(pairs)]
    late = [jnp.concatenate(second[2 * at : 2 * at + 2], axis=1) for at in range(pairs)]
    total = [None] * pairs
    for d in range(pairs):
        matrix = jnp.concatenate(
            [
                jnp.concatenate([band_ref[2 * d + 1], band_ref[2 * d + 2]], axis=1),
                jnp.concatenate([band_ref[2 * d], band_ref[2 * d + 1]], axis=1),
            ],
            axis=0,
        )
        if d:
            used = [jnp.where(after[n + d], late[n], full[n]) for n in range(pairs - d)]
        else:
            used = full + late
        result = jnp.dot(jnp.concatenate(used, axis=0), matrix, preferred_element_type=F32)
        pieces = [result[n * CH : (n + 1) * CH] for n in range(len(used))]
        if d:
            for n in range(pairs - d):
                total[n + d] = total[n + d] + pieces[n]
        else:
            total, alone = pieces[:pairs], pieces[pairs:]
    for a in range(NB):
        side = slice((a % 2) * TB, (a % 2 + 1) * TB)
        inner = masks[a] & ~after[a // 2][:, side]
        conv = jnp.where(inner, alone[a // 2][:, side], total[a // 2][:, side])
        out_ref[a] = (conv + weight_ref[6] * product[a].astype(F32)).astype(BF16)


def square_kernel(u_ref, gate_ref, x_ref, row_ref, part_ref, turned_ref):
    halo = x_ref[0, HALO:, :].astype(F32)
    for n in range(1, NB):
        halo = halo + x_ref[n, HALO:, :].astype(F32)
    row_at = lax.broadcasted_iota(jnp.int32, (TB, TB), 0)
    squares = jnp.zeros((1, TB), F32)
    for n in range(4):
        lanes = slice(n * TB, (n + 1) * TB)
        older, last = halo[2 * n : 2 * n + 1], halo[2 * n + 1 : 2 * n + 2]
        zero = row_ref[1:2, lanes] * last + row_ref[2:3, lanes] * older
        one = row_ref[2:3, lanes] * last
        extra = jnp.where(row_at == 0, zero, jnp.where(row_at == 1, one, 0.0)).T
        gated = u_ref[lanes, :].astype(F32) * (gate_ref[lanes, :] + extra)
        squares = squares + jnp.sum(gated * gated, axis=0, keepdims=True)
        turned_ref[:, lanes] = gated.T * row_ref[3:4, lanes]
    part_ref[...] = jnp.broadcast_to(squares, (NB, 1, TB))


def finish_kernel(x_ref, part_ref, out_ref):
    squares = jnp.sum(part_ref[...], axis=0)
    scale = lax.rsqrt(squares / D + 1e-06)
    scale = jnp.broadcast_to(scale, (TB, TB)).T
    for n in range(4):
        lanes = slice(n * TB, (n + 1) * TB)
        out_ref[:, lanes] = (x_ref[:, lanes] * scale).astype(BF16)


VM = pl.BlockSpec(memory_space=pltpu.VMEM)
SM = pl.BlockSpec(memory_space=pltpu.SMEM)


def keep(value):
    return pltpu.with_memory_space_constraint(value, pltpu.VMEM)


def on_device(q_in, k_in, v_in, fir, skip, taps, segments, gain):
    width = q_in.shape[1]
    payload, band, weight, gate, rows = pl.pallas_call(
        prepare_kernel,
        out_shape=(
            pltpu.VMEM((NB, ROWS, TB), BF16),
            pltpu.VMEM((NB + 1, TB, TB), BF16),
            pltpu.VMEM((7, CH, TB), F32),
            pltpu.VMEM((width, TB), F32),
            pltpu.VMEM((8, width), F32),
        ),
        in_specs=[VM] * 8,
        out_specs=(VM,) * 5,
        scratch_shapes=[pltpu.VMEM((GW, GW), F32)],
        name="prepare",
    )(
        k_in, v_in, q_in, segments.reshape(1, TB),
        fir, skip.reshape(1, width), taps, gain.reshape(1, width),
    )
    payload = lax.all_to_all(payload, "ctx", 0, 0, tiled=True)
    mixed = pl.pallas_call(
        conv_kernel,
        out_shape=pltpu.VMEM((NB, CH, TB), BF16),
        in_specs=[VM] * 3,
        out_specs=VM,
        name="conv",
    )(keep(payload), keep(band), keep(weight))
    mixed = lax.all_to_all(mixed, "ctx", 0, 0, tiled=True).reshape(width, TB)
    part, turned = pl.pallas_call(
        square_kernel,
        out_shape=(pltpu.VMEM((NB, 1, TB), F32), pltpu.VMEM((TB, width), F32)),
        in_specs=[VM] * 4,
        out_specs=(VM,) * 2,
        name="squares",
    )(keep(mixed), keep(gate), keep(payload), keep(rows))
    part = lax.all_to_all(part, "grp", 0, 0, tiled=True)
    return pl.pallas_call(
        finish_kernel,
        out_shape=jax.ShapeDtypeStruct((TB, width), BF16),
        in_specs=[VM] * 2,
        out_specs=VM,
        name="finish",
    )(keep(turned), keep(part))


def solution(mesh):
    return jax.shard_map(
        on_device,
        mesh=mesh,
        in_specs=(
            P("ctx", "grp"),
            P("ctx", "grp"),
            P("ctx", "grp"),
            P(None, None, "grp"),
            P("grp"),
            P("grp", None),
            P("ctx"),
            P("grp"),
        ),
        out_specs=P("ctx", "grp"),
        check_vma=False,
    )
```

```python
import jax
import jax.numpy as jnp
from jax import lax
from jax.experimental import pallas as pl
from jax.experimental.pallas import tpu as pltpu
from jax.sharding import PartitionSpec as P

D = 8192
GW = 128
NB = 16
TB = 128
CH = 32
HALO = CH
EDGE = HALO + 8
ROWS = HALO + 16
CTX_ORDER = [(10 + n) % NB for n in range(NB)]
GRP_ORDER = [(9 + n) % NB for n in range(NB)]
PLACE = [CTX_ORDER.index(a) for a in range(NB)]
F32 = jnp.float32
BF16 = jnp.bfloat16


def fir_filter(ref, fir_ref, which, lanes, row_at=None):
    value = ref[:, lanes].astype(F32)
    one, two = pltpu.roll(value, 1, 0), pltpu.roll(value, 2, 0)
    if row_at is not None:
        one, two = jnp.where(row_at == 0, 0.0, one), jnp.where(row_at <= 1, 0.0, two)
    taps = [fir_ref[which, n : n + 1, lanes] for n in range(3)]
    return taps[0] * value + taps[1] * one + taps[2] * two


def prepare_kernel(
    k_ref, v_ref, q_ref, seg_ref, fir_ref, skip_ref, taps_ref, gain_ref,
    out_ref, band_ref, weight_ref, gate_ref, row_ref, coef_ref,
):
    index = lax.axis_index("ctx")
    row_at = lax.broadcasted_iota(jnp.int32, (TB, TB), 0)
    col_at = lax.broadcasted_iota(jnp.int32, (TB, TB), 1)
    same = jnp.where(row_at == col_at, 1.0, 0.0).astype(BF16)
    first = jnp.sum(jnp.where(seg_ref[...] == 0, 1.0, 0.0), axis=1, keepdims=True)
    tail = q_ref[TB - 16 :, :].astype(F32)[14:16]
    tail = jnp.concatenate([tail[:, n * TB : (n + 1) * TB] for n in range(4)], axis=0)
    heads = [ref[0:16, :].astype(F32)[0:2] for ref in (k_ref, v_ref)]
    tails = [ref[TB - 16 :, :].astype(F32)[14:16] for ref in (k_ref, v_ref)]
    edges = jnp.concatenate([heads[0], tails[0], heads[1], tails[1]], axis=0)
    for n in range(4):
        lanes = slice(n * TB, (n + 1) * TB)
        value = fir_filter(k_ref, fir_ref, 1, lanes) * fir_filter(v_ref, fir_ref, 2, lanes)
        value = lax.dot_general(
            same, value.astype(BF16), (((1,), (1,)), ((), ())), preferred_element_type=F32
        )
        value = jnp.where(col_at == 0, first, value).astype(BF16)
        gate_ref[lanes, :] = fir_filter(q_ref, fir_ref, 0, lanes, row_at).T
        for m in range(4):
            here = jnp.where(index == 4 * n + m - 1, tail, 0.0)
            edge = pltpu.roll(edges[:, lanes], (TB - m * CH) % TB, 1) if m else edges[:, lanes]
            at = PLACE[4 * n + m]
            out_ref[at, 0:CH, :] = value[m * CH : (m + 1) * CH]
            out_ref[at, HALO:, :] = jnp.concatenate([here, edge], axis=0).astype(BF16)

    tile = pl.multiple_of((index // 4) * GW, GW)
    rows = [fir_ref[a, :, pl.ds(tile, GW)] for a in (1, 2)]
    rows.append(skip_ref[:, pl.ds(tile, GW)])
    rows.append(jnp.zeros((1, GW), F32))
    coef_ref[:, 0:8] = jnp.concatenate(rows, axis=0).T
    coef = coef_ref[pl.ds(pl.multiple_of((index % 4) * CH, CH), CH), :]
    for n in range(7):
        weight_ref[n] = jnp.broadcast_to(coef[:, n : n + 1], (CH, TB))
    row_ref[0:3] = fir_ref[0]
    row_ref[3:4] = gain_ref[...]

    taps = taps_ref[...].astype(F32)
    pick = lax.broadcasted_iota(jnp.int32, taps.shape, 0) == index // 4
    row = jnp.sum(jnp.where(pick, taps, 0.0), axis=0, keepdims=True)
    upper = col_at >= row_at
    before = jnp.zeros((TB, TB), F32)
    band_ref[0] = before.astype(BF16)
    for m in range(NB):
        piece = jnp.broadcast_to(row[:, m * TB : (m + 1) * TB], (TB, TB))
        rolled = pltpu.roll(piece, 0, 1, stride=1, stride_axis=0)
        band_ref[m + 1] = jnp.where(upper, rolled, before).astype(BF16)
        before = rolled


def conv_kernel(x_ref, band_ref, weight_ref, out_ref):
    lane = lax.broadcasted_iota(jnp.int32, (CH, TB), 1)
    edges = jnp.concatenate([x_ref[PLACE[a], HALO:, :].astype(F32)[8:16] for a in range(NB)], axis=0).T[0:CH]

    def ahead(by):
        return pltpu.roll(edges, TB - by, 1) if by else edges

    def behind(by):
        return jnp.where(lane < 8, 0.0, pltpu.roll(edges, by, 1))

    def pair(at, which):
        w = [weight_ref[3 * which + n] for n in range(3)]
        zero, one, older, last = ahead(at), ahead(at + 1), behind(6 - at), behind(5 - at)
        return w[0] * zero + w[1] * last + w[2] * older, w[0] * one + w[1] * zero + w[2] * last

    k_zero, k_one = pair(0, 0)
    v_zero, v_one = pair(4, 1)
    fixed = jnp.where(lane % 8 == 0, k_zero * v_zero, pltpu.roll(k_one * v_one, 1, 1))

    product, second, masks, after = [], [], [], []
    for a in range(NB):
        value = x_ref[PLACE[a], 0:CH, :].astype(F32)
        first = jnp.broadcast_to(value[:, 0:1], (CH, TB))
        mask = lane.astype(F32) >= first
        if a % 2 == 0:
            after.append(jnp.concatenate([first, first], axis=1) == 0.0)
        value = jnp.where(lane < 2, pltpu.roll(fixed, (TB - 8 * a) % TB, 1) if a else fixed, value)
        product.append(value.astype(BF16))
        second.append(jnp.where(mask, value, 0.0).astype(BF16))
        masks.append(mask)
    pairs = NB // 2
    full = [jnp.concatenate(product[2 * at : 2 * at + 2], axis=1) for at in range(pairs)]
    late = [jnp.concatenate(second[2 * at : 2 * at + 2], axis=1) for at in range(pairs)]
    total = [None] * pairs
    for d in range(pairs):
        matrix = jnp.concatenate(
            [
                jnp.concatenate([band_ref[2 * d + 1], band_ref[2 * d + 2]], axis=1),
                jnp.concatenate([band_ref[2 * d], band_ref[2 * d + 1]], axis=1),
            ],
            axis=0,
        )
        if d:
            used = [jnp.where(after[n + d], late[n], full[n]) for n in range(pairs - d)]
        else:
            used = full + late
        result = jnp.dot(jnp.concatenate(used, axis=0), matrix, preferred_element_type=F32)
        pieces = [result[n * CH : (n + 1) * CH] for n in range(len(used))]
        if d:
            for n in range(pairs - d):
                total[n + d] = total[n + d] + pieces[n]
        else:
            total, alone = pieces[:pairs], pieces[pairs:]
    for a in range(NB):
        side = slice((a % 2) * TB, (a % 2 + 1) * TB)
        inner = masks[a] & ~after[a // 2][:, side]
        conv = jnp.where(inner, alone[a // 2][:, side], total[a // 2][:, side])
        out_ref[PLACE[a]] = (conv + weight_ref[6] * product[a].astype(F32)).astype(BF16)


def square_kernel(u_ref, gate_ref, x_ref, row_ref, part_ref, turned_ref):
    halo = x_ref[0, HALO:, :].astype(F32)
    for n in range(1, NB):
        halo = halo + x_ref[n, HALO:, :].astype(F32)
    row_at = lax.broadcasted_iota(jnp.int32, (TB, TB), 0)
    squares = jnp.zeros((1, TB), F32)
    for n in range(4):
        lanes = slice(n * TB, (n + 1) * TB)
        older, last = halo[2 * n : 2 * n + 1], halo[2 * n + 1 : 2 * n + 2]
        zero = row_ref[1:2, lanes] * last + row_ref[2:3, lanes] * older
        one = row_ref[2:3, lanes] * last
        extra = jnp.where(row_at == 0, zero, jnp.where(row_at == 1, one, 0.0)).T
        mixed = jnp.concatenate([u_ref[PLACE[4 * n + m]] for m in range(4)], axis=0)
        gated = mixed.astype(F32) * (gate_ref[lanes, :] + extra)
        squares = squares + jnp.sum(gated * gated, axis=0, keepdims=True)
        turned_ref[:, lanes] = gated.T * row_ref[3:4, lanes]
    part_ref[...] = jnp.broadcast_to(squares, (NB, 1, TB))


def finish_kernel(x_ref, part_ref, out_ref):
    squares = jnp.sum(part_ref[...], axis=0)
    scale = lax.rsqrt(squares / D + 1e-06)
    scale = jnp.broadcast_to(scale, (TB, TB)).T
    for n in range(4):
        lanes = slice(n * TB, (n + 1) * TB)
        out_ref[:, lanes] = (x_ref[:, lanes] * scale).astype(BF16)


VM = pl.BlockSpec(memory_space=pltpu.VMEM)
SM = pl.BlockSpec(memory_space=pltpu.SMEM)


def keep(value):
    return pltpu.with_memory_space_constraint(value, pltpu.VMEM)


def exchange(value, axis, order):
    return lax.all_to_all(value, axis, 0, 0, axis_index_groups=[order], tiled=True)


def on_device(q_in, k_in, v_in, fir, skip, taps, segments, gain):
    width = q_in.shape[1]
    payload, band, weight, gate, rows = pl.pallas_call(
        prepare_kernel,
        out_shape=(
            pltpu.VMEM((NB, ROWS, TB), BF16),
            pltpu.VMEM((NB + 1, TB, TB), BF16),
            pltpu.VMEM((7, CH, TB), F32),
            pltpu.VMEM((width, TB), F32),
            pltpu.VMEM((8, width), F32),
        ),
        in_specs=[VM] * 8,
        out_specs=(VM,) * 5,
        scratch_shapes=[pltpu.VMEM((GW, GW), F32)],
        name="prepare",
    )(
        k_in, v_in, q_in, segments.reshape(1, TB),
        fir, skip.reshape(1, width), taps, gain.reshape(1, width),
    )
    payload = exchange(payload, "ctx", CTX_ORDER)
    mixed = pl.pallas_call(
        conv_kernel,
        out_shape=pltpu.VMEM((NB, CH, TB), BF16),
        in_specs=[VM] * 3,
        out_specs=VM,
        name="conv",
    )(keep(payload), keep(band), keep(weight))
    mixed = exchange(mixed, "ctx", CTX_ORDER)
    part, turned = pl.pallas_call(
        square_kernel,
        out_shape=(pltpu.VMEM((NB, 1, TB), F32), pltpu.VMEM((TB, width), F32)),
        in_specs=[VM] * 4,
        out_specs=(VM,) * 2,
        name="squares",
    )(keep(mixed), keep(gate), keep(payload), keep(rows))
    part = exchange(part, "grp", GRP_ORDER)
    return pl.pallas_call(
        finish_kernel,
        out_shape=jax.ShapeDtypeStruct((TB, width), BF16),
        in_specs=[VM] * 2,
        out_specs=VM,
        name="finish",
    )(keep(turned), keep(part))


def solution(mesh):
    return jax.shard_map(
        on_device,
        mesh=mesh,
        in_specs=(
            P("ctx", "grp"),
            P("ctx", "grp"),
            P("ctx", "grp"),
            P(None, None, "grp"),
            P("grp"),
            P("grp", None),
            P("ctx"),
            P("grp"),
        ),
        out_specs=P("ctx", "grp"),
        check_vma=False,
    )
```

```python
import jax
import jax.numpy as jnp
from jax import lax
from jax.experimental import pallas as pl
from jax.experimental.pallas import tpu as pltpu
from jax.sharding import PartitionSpec as P

D = 8192
GW = 128
NB = 16
TB = 128
CH = 32
HALO = CH
EDGE = HALO + 8
ROWS = HALO + 16
CTX_ORDER = [(10 + n) % NB for n in range(NB)]
GRP_ORDER = [(9 + n) % NB for n in range(NB)]
PLACE = [CTX_ORDER.index(a) for a in range(NB)]
F32 = jnp.float32
BF16 = jnp.bfloat16


def fir_filter(ref, fir_ref, which, lanes, row_at=None):
    value = ref[:, lanes].astype(F32)
    one, two = pltpu.roll(value, 1, 0), pltpu.roll(value, 2, 0)
    if row_at is not None:
        one, two = jnp.where(row_at == 0, 0.0, one), jnp.where(row_at <= 1, 0.0, two)
    taps = [fir_ref[which, n : n + 1, lanes] for n in range(3)]
    return taps[0] * value + taps[1] * one + taps[2] * two


def prepare_kernel(
    k_ref, v_ref, q_ref, seg_ref, fir_ref, skip_ref, taps_ref, gain_ref,
    out_ref, band_ref, weight_ref, gate_ref, row_ref, coef_ref,
):
    index = lax.axis_index("ctx")
    row_at = lax.broadcasted_iota(jnp.int32, (TB, TB), 0)
    col_at = lax.broadcasted_iota(jnp.int32, (TB, TB), 1)
    taps = taps_ref[...].astype(F32)
    pick = lax.broadcasted_iota(jnp.int32, taps.shape, 0) == index // 4
    row = jnp.sum(jnp.where(pick, taps, 0.0), axis=0, keepdims=True)
    upper = col_at >= row_at
    before = jnp.zeros((TB, TB), F32)
    band_ref[0] = before.astype(BF16)
    for m in range(NB):
        piece = jnp.broadcast_to(row[:, m * TB : (m + 1) * TB], (TB, TB))
        rolled = pltpu.roll(piece, 0, 1, stride=1, stride_axis=0)
        band_ref[m + 1] = jnp.where(upper, rolled, before).astype(BF16)
        before = rolled
    same = jnp.where(row_at == col_at, 1.0, 0.0).astype(BF16)
    first = jnp.sum(jnp.where(seg_ref[...] == 0, 1.0, 0.0), axis=1, keepdims=True)
    tail = q_ref[TB - 16 :, :].astype(F32)[14:16]
    tail = jnp.concatenate([tail[:, n * TB : (n + 1) * TB] for n in range(4)], axis=0)
    heads = [ref[0:16, :].astype(F32)[0:2] for ref in (k_ref, v_ref)]
    tails = [ref[TB - 16 :, :].astype(F32)[14:16] for ref in (k_ref, v_ref)]
    edges = jnp.concatenate([heads[0], tails[0], heads[1], tails[1]], axis=0)
    for n in range(4):
        lanes = slice(n * TB, (n + 1) * TB)
        value = fir_filter(k_ref, fir_ref, 1, lanes) * fir_filter(v_ref, fir_ref, 2, lanes)
        value = lax.dot_general(
            same, value.astype(BF16), (((1,), (1,)), ((), ())), preferred_element_type=F32
        )
        value = jnp.where(col_at == 0, first, value).astype(BF16)
        gate_ref[lanes, :] = fir_filter(q_ref, fir_ref, 0, lanes, row_at).T
        for m in range(4):
            here = jnp.where(index == 4 * n + m - 1, tail, 0.0)
            edge = pltpu.roll(edges[:, lanes], (TB - m * CH) % TB, 1) if m else edges[:, lanes]
            at = PLACE[4 * n + m]
            out_ref[at, 0:CH, :] = value[m * CH : (m + 1) * CH]
            out_ref[at, HALO:, :] = jnp.concatenate([here, edge], axis=0).astype(BF16)

    tile = pl.multiple_of((index // 4) * GW, GW)
    rows = [fir_ref[a, :, pl.ds(tile, GW)] for a in (1, 2)]
    rows.append(skip_ref[:, pl.ds(tile, GW)])
    rows.append(jnp.zeros((1, GW), F32))
    coef_ref[:, 0:8] = jnp.concatenate(rows, axis=0).T
    coef = coef_ref[pl.ds(pl.multiple_of((index % 4) * CH, CH), CH), :]
    for n in range(7):
        weight_ref[n] = jnp.broadcast_to(coef[:, n : n + 1], (CH, TB))
    row_ref[0:3] = fir_ref[0]
    row_ref[3:4] = gain_ref[...]


def conv_kernel(x_ref, band_ref, weight_ref, out_ref):
    lane = lax.broadcasted_iota(jnp.int32, (CH, TB), 1)
    edges = jnp.concatenate([x_ref[PLACE[a], HALO:, :].astype(F32)[8:16] for a in range(NB)], axis=0).T[0:CH]

    def ahead(by):
        return pltpu.roll(edges, TB - by, 1) if by else edges

    def behind(by):
        return jnp.where(lane < 8, 0.0, pltpu.roll(edges, by, 1))

    def pair(at, which):
        w = [weight_ref[3 * which + n] for n in range(3)]
        zero, one, older, last = ahead(at), ahead(at + 1), behind(6 - at), behind(5 - at)
        return w[0] * zero + w[1] * last + w[2] * older, w[0] * one + w[1] * zero + w[2] * last

    k_zero, k_one = pair(0, 0)
    v_zero, v_one = pair(4, 1)
    fixed = jnp.where(lane % 8 == 0, k_zero * v_zero, pltpu.roll(k_one * v_one, 1, 1))

    product, second, masks, after = [], [], [], []
    for a in range(NB):
        value = x_ref[PLACE[a], 0:CH, :].astype(F32)
        first = jnp.broadcast_to(value[0:8, 0:1], (8, TB))
        first = jnp.concatenate([first] * 4, axis=0)
        mask = lane.astype(F32) >= first
        if a % 2 == 0:
            after.append(jnp.concatenate([first, first], axis=1) == 0.0)
        value = jnp.where(lane < 2, pltpu.roll(fixed, (TB - 8 * a) % TB, 1) if a else fixed, value)
        product.append(value.astype(BF16))
        second.append(jnp.where(mask, value, 0.0).astype(BF16))
        masks.append(mask)
    pairs = NB // 2
    full = [jnp.concatenate(product[2 * at : 2 * at + 2], axis=1) for at in range(pairs)]
    late = [jnp.concatenate(second[2 * at : 2 * at + 2], axis=1) for at in range(pairs)]
    total = [None] * pairs
    for d in range(pairs):
        matrix = jnp.concatenate(
            [
                jnp.concatenate([band_ref[2 * d + 1], band_ref[2 * d + 2]], axis=1),
                jnp.concatenate([band_ref[2 * d], band_ref[2 * d + 1]], axis=1),
            ],
            axis=0,
        )
        if d:
            used = [jnp.where(after[n + d], late[n], full[n]) for n in range(pairs - d)]
        else:
            used = full + late
        result = jnp.dot(jnp.concatenate(used, axis=0), matrix, preferred_element_type=F32)
        pieces = [result[n * CH : (n + 1) * CH] for n in range(len(used))]
        if d:
            for n in range(pairs - d):
                total[n + d] = total[n + d] + pieces[n]
        else:
            total, alone = pieces[:pairs], pieces[pairs:]
    for a in range(NB):
        side = slice((a % 2) * TB, (a % 2 + 1) * TB)
        inner = masks[a] & ~after[a // 2][:, side]
        conv = jnp.where(inner, alone[a // 2][:, side], total[a // 2][:, side])
        out_ref[PLACE[a]] = (conv + weight_ref[6] * product[a].astype(F32)).astype(BF16)


def square_kernel(u_ref, gate_ref, x_ref, row_ref, part_ref, turned_ref):
    halo = x_ref[0, HALO:, :].astype(F32)
    for n in range(1, NB):
        halo = halo + x_ref[n, HALO:, :].astype(F32)
    row_at = lax.broadcasted_iota(jnp.int32, (TB, TB), 0)
    squares = jnp.zeros((1, TB), F32)
    for n in range(4):
        lanes = slice(n * TB, (n + 1) * TB)
        older, last = halo[2 * n : 2 * n + 1], halo[2 * n + 1 : 2 * n + 2]
        zero = row_ref[1:2, lanes] * last + row_ref[2:3, lanes] * older
        one = row_ref[2:3, lanes] * last
        extra = jnp.where(row_at == 0, zero, jnp.where(row_at == 1, one, 0.0)).T
        mixed = jnp.concatenate([u_ref[PLACE[4 * n + m]] for m in range(4)], axis=0)
        gated = mixed.astype(F32) * (gate_ref[lanes, :] + extra)
        squares = squares + jnp.sum(gated * gated, axis=0, keepdims=True)
        turned_ref[:, lanes] = gated.T * row_ref[3:4, lanes]
    part_ref[...] = jnp.broadcast_to(squares, (NB, 1, TB))


def finish_kernel(x_ref, part_ref, out_ref):
    squares = jnp.sum(part_ref[...], axis=0)
    scale = lax.rsqrt(squares / D + 1e-06)
    scale = jnp.broadcast_to(scale, (TB, TB)).T
    for n in range(4):
        lanes = slice(n * TB, (n + 1) * TB)
        out_ref[:, lanes] = (x_ref[:, lanes] * scale).astype(BF16)


VM = pl.BlockSpec(memory_space=pltpu.VMEM)
SM = pl.BlockSpec(memory_space=pltpu.SMEM)


def keep(value):
    return pltpu.with_memory_space_constraint(value, pltpu.VMEM)


def exchange(value, axis, order):
    return lax.all_to_all(value, axis, 0, 0, axis_index_groups=[order], tiled=True)


def on_device(q_in, k_in, v_in, fir, skip, taps, segments, gain):
    width = q_in.shape[1]
    payload, band, weight, gate, rows = pl.pallas_call(
        prepare_kernel,
        out_shape=(
            pltpu.VMEM((NB, ROWS, TB), BF16),
            pltpu.VMEM((NB + 1, TB, TB), BF16),
            pltpu.VMEM((7, CH, TB), F32),
            pltpu.VMEM((width, TB), F32),
            pltpu.VMEM((8, width), F32),
        ),
        in_specs=[VM] * 8,
        out_specs=(VM,) * 5,
        scratch_shapes=[pltpu.VMEM((GW, GW), F32)],
        name="prepare",
    )(
        k_in, v_in, q_in, segments.reshape(1, TB),
        fir, skip.reshape(1, width), taps, gain.reshape(1, width),
    )
    payload = exchange(payload, "ctx", CTX_ORDER)
    mixed = pl.pallas_call(
        conv_kernel,
        out_shape=pltpu.VMEM((NB, CH, TB), BF16),
        in_specs=[VM] * 3,
        out_specs=VM,
        name="conv",
    )(keep(payload), keep(band), keep(weight))
    mixed = exchange(mixed, "ctx", CTX_ORDER)
    part, turned = pl.pallas_call(
        square_kernel,
        out_shape=(pltpu.VMEM((NB, 1, TB), F32), pltpu.VMEM((TB, width), F32)),
        in_specs=[VM] * 4,
        out_specs=(VM,) * 2,
        name="squares",
    )(keep(mixed), keep(gate), keep(payload), keep(rows))
    part = exchange(part, "grp", GRP_ORDER)
    return pl.pallas_call(
        finish_kernel,
        out_shape=jax.ShapeDtypeStruct((TB, width), BF16),
        in_specs=[VM] * 2,
        out_specs=VM,
        name="finish",
    )(keep(turned), keep(part))


def solution(mesh):
    return jax.shard_map(
        on_device,
        mesh=mesh,
        in_specs=(
            P("ctx", "grp"),
            P("ctx", "grp"),
            P("ctx", "grp"),
            P(None, None, "grp"),
            P("grp"),
            P("grp", None),
            P("ctx"),
            P("grp"),
        ),
        out_specs=P("ctx", "grp"),
        check_vma=False,
    )
```

```python
import jax
import jax.numpy as jnp
from jax import lax
from jax.experimental import pallas as pl
from jax.experimental.pallas import tpu as pltpu
from jax.sharding import PartitionSpec as P

D = 8192
GW = 128
NB = 16
TB = 128
CH = 32
HALO = CH
EDGE = HALO + 8
ROWS = HALO + 16
CTX_ORDER = [(10 + n) % NB for n in range(NB)]
GRP_ORDER = [(9 + n) % NB for n in range(NB)]
PLACE = [CTX_ORDER.index(a) for a in range(NB)]
F32 = jnp.float32
BF16 = jnp.bfloat16


def fir_filter(ref, taps, lanes, row_at=None):
    value = ref[:, lanes].astype(F32)
    one, two = pltpu.roll(value, 1, 0), pltpu.roll(value, 2, 0)
    if row_at is not None:
        one, two = jnp.where(row_at == 0, 0.0, one), jnp.where(row_at <= 1, 0.0, two)
    return taps[0] * value + taps[1] * one + taps[2] * two


def prepare_kernel(*refs):
    sources, outs, coef_ref, sems = refs[:8], refs[8:13], refs[20], refs[21]
    buffers = refs[13:16] + refs[12:13] + refs[16:20]
    taps_ref, k_ref, v_ref, q_ref, fir_ref, skip_ref, gain_ref, seg_ref = buffers
    out_ref, band_ref, weight_ref, row_ref = outs[:4]
    copies = [pltpu.make_async_copy(src, dst, sems.at[n]) for n, (src, dst) in enumerate(zip(sources, buffers))]
    for copy in copies:
        copy.start()
    index = lax.axis_index("ctx")
    row_at = lax.broadcasted_iota(jnp.int32, (TB, TB), 0)
    col_at = lax.broadcasted_iota(jnp.int32, (TB, TB), 1)
    copies[0].wait()
    taps = taps_ref[...].astype(F32)
    pick = lax.broadcasted_iota(jnp.int32, taps.shape, 0) == index // 4
    row = jnp.sum(jnp.where(pick, taps, 0.0), axis=0, keepdims=True)
    upper = col_at >= row_at
    before = jnp.zeros((TB, TB), F32)
    band_ref[0] = before.astype(BF16)
    for m in range(NB):
        piece = jnp.broadcast_to(row[:, m * TB : (m + 1) * TB], (TB, TB))
        rolled = pltpu.roll(piece, 0, 1, stride=1, stride_axis=0)
        band_ref[m + 1] = jnp.where(upper, rolled, before).astype(BF16)
        before = rolled
    for copy in copies[1:]:
        copy.wait()
    same = jnp.where(row_at == col_at, 1.0, 0.0).astype(BF16)
    first = jnp.sum(jnp.where(seg_ref[...] == 0, 1.0, 0.0), axis=1, keepdims=True)
    tail = q_ref[TB - 16 :, :].astype(F32)[14:16]
    tail = jnp.concatenate([tail[:, n * TB : (n + 1) * TB] for n in range(4)], axis=0)
    heads = [ref[0:16, :].astype(F32)[0:2] for ref in (k_ref, v_ref)]
    tails = [ref[TB - 16 :, :].astype(F32)[14:16] for ref in (k_ref, v_ref)]
    edges = jnp.concatenate([heads[0], tails[0], heads[1], tails[1]], axis=0)
    for n in range(4):
        lanes = slice(n * TB, (n + 1) * TB)
        k_taps, v_taps = ([fir_ref[a, m : m + 1, lanes] for m in range(3)] for a in (1, 2))
        value = fir_filter(k_ref, k_taps, lanes) * fir_filter(v_ref, v_taps, lanes)
        value = lax.dot_general(
            same, value.astype(BF16), (((1,), (1,)), ((), ())), preferred_element_type=F32
        )
        value = jnp.where(col_at == 0, first, value).astype(BF16)
        for m in range(4):
            here = jnp.where(index == 4 * n + m - 1, tail, 0.0)
            edge = pltpu.roll(edges[:, lanes], (TB - m * CH) % TB, 1) if m else edges[:, lanes]
            at = PLACE[4 * n + m]
            out_ref[at, 0:CH, :] = value[m * CH : (m + 1) * CH]
            out_ref[at, HALO:, :] = jnp.concatenate([here, edge], axis=0).astype(BF16)

    tile = pl.multiple_of((index // 4) * GW, GW)
    rows = [fir_ref[a, :, pl.ds(tile, GW)] for a in (1, 2)]
    rows.append(skip_ref[:, pl.ds(tile, GW)])
    rows.append(jnp.zeros((1, GW), F32))
    coef_ref[:, 0:8] = jnp.concatenate(rows, axis=0).T
    coef = coef_ref[pl.ds(pl.multiple_of((index % 4) * CH, CH), CH), :]
    for n in range(7):
        weight_ref[n] = jnp.broadcast_to(coef[:, n : n + 1], (CH, TB))
    row_ref[0:3] = fir_ref[0]
    row_ref[3:4] = gain_ref[...]


def conv_kernel(x_ref, band_ref, weight_ref, q_ref, row_ref, out_ref, gate_ref):
    row_at = lax.broadcasted_iota(jnp.int32, (TB, TB), 0)
    for n in range(4):
        lanes = slice(n * TB, (n + 1) * TB)
        gate_ref[lanes, :] = fir_filter(q_ref, [row_ref[m : m + 1, lanes] for m in range(3)], lanes, row_at).T
    lane = lax.broadcasted_iota(jnp.int32, (CH, TB), 1)
    edges = jnp.concatenate([x_ref[PLACE[a], HALO:, :].astype(F32)[8:16] for a in range(NB)], axis=0).T[0:CH]

    def ahead(by):
        return pltpu.roll(edges, TB - by, 1) if by else edges

    def behind(by):
        return jnp.where(lane < 8, 0.0, pltpu.roll(edges, by, 1))

    def pair(at, which):
        w = [weight_ref[3 * which + n] for n in range(3)]
        zero, one, older, last = ahead(at), ahead(at + 1), behind(6 - at), behind(5 - at)
        return w[0] * zero + w[1] * last + w[2] * older, w[0] * one + w[1] * zero + w[2] * last

    k_zero, k_one = pair(0, 0)
    v_zero, v_one = pair(4, 1)
    fixed = jnp.where(lane % 8 == 0, k_zero * v_zero, pltpu.roll(k_one * v_one, 1, 1))

    product, second, masks, after = [], [], [], []
    for a in range(NB):
        value = x_ref[PLACE[a], 0:CH, :].astype(F32)
        first = jnp.broadcast_to(value[0:8, 0:1], (8, TB))
        first = jnp.concatenate([first] * 4, axis=0)
        mask = lane.astype(F32) >= first
        if a % 2 == 0:
            after.append(jnp.concatenate([first, first], axis=1) == 0.0)
        value = jnp.where(lane < 2, pltpu.roll(fixed, (TB - 8 * a) % TB, 1) if a else fixed, value)
        product.append(value.astype(BF16))
        second.append(jnp.where(mask, value, 0.0).astype(BF16))
        masks.append(mask)
    pairs = NB // 2
    full = [jnp.concatenate(product[2 * at : 2 * at + 2], axis=1) for at in range(pairs)]
    late = [jnp.concatenate(second[2 * at : 2 * at + 2], axis=1) for at in range(pairs)]
    total = [None] * pairs
    for d in range(pairs):
        matrix = jnp.concatenate(
            [
                jnp.concatenate([band_ref[2 * d + 1], band_ref[2 * d + 2]], axis=1),
                jnp.concatenate([band_ref[2 * d], band_ref[2 * d + 1]], axis=1),
            ],
            axis=0,
        )
        if d:
            used = [jnp.where(after[n + d], late[n], full[n]) for n in range(pairs - d)]
        else:
            used = full + late
        result = jnp.dot(jnp.concatenate(used, axis=0), matrix, preferred_element_type=F32)
        pieces = [result[n * CH : (n + 1) * CH] for n in range(len(used))]
        if d:
            for n in range(pairs - d):
                total[n + d] = total[n + d] + pieces[n]
        else:
            total, alone = pieces[:pairs], pieces[pairs:]
    for a in range(NB):
        side = slice((a % 2) * TB, (a % 2 + 1) * TB)
        inner = masks[a] & ~after[a // 2][:, side]
        conv = jnp.where(inner, alone[a // 2][:, side], total[a // 2][:, side])
        out_ref[PLACE[a]] = (conv + weight_ref[6] * product[a].astype(F32)).astype(BF16)


def square_kernel(u_ref, gate_ref, x_ref, row_ref, part_ref, turned_ref):
    halo = x_ref[0, HALO:, :].astype(F32)
    for n in range(1, NB):
        halo = halo + x_ref[n, HALO:, :].astype(F32)
    row_at = lax.broadcasted_iota(jnp.int32, (TB, TB), 0)
    squares = jnp.zeros((1, TB), F32)
    for n in range(4):
        lanes = slice(n * TB, (n + 1) * TB)
        older, last = halo[2 * n : 2 * n + 1], halo[2 * n + 1 : 2 * n + 2]
        zero = row_ref[1:2, lanes] * last + row_ref[2:3, lanes] * older
        one = row_ref[2:3, lanes] * last
        extra = jnp.where(row_at == 0, zero, jnp.where(row_at == 1, one, 0.0)).T
        mixed = jnp.concatenate([u_ref[PLACE[4 * n + m]] for m in range(4)], axis=0)
        gated = mixed.astype(F32) * (gate_ref[lanes, :] + extra)
        squares = squares + jnp.sum(gated * gated, axis=0, keepdims=True)
        turned_ref[:, lanes] = gated.T * row_ref[3:4, lanes]
    part_ref[...] = jnp.broadcast_to(squares, (NB, 1, TB))


def finish_kernel(x_ref, part_ref, out_ref):
    squares = jnp.sum(part_ref[...], axis=0)
    scale = lax.rsqrt(squares / D + 1e-06)
    scale = jnp.broadcast_to(scale, (TB, TB)).T
    for n in range(4):
        lanes = slice(n * TB, (n + 1) * TB)
        out_ref[:, lanes] = (x_ref[:, lanes] * scale).astype(BF16)


VM = pl.BlockSpec(memory_space=pltpu.VMEM)
SM = pl.BlockSpec(memory_space=pltpu.SMEM)


def keep(value):
    return pltpu.with_memory_space_constraint(value, pltpu.VMEM)


def exchange(value, axis, order):
    return lax.all_to_all(value, axis, 0, 0, axis_index_groups=[order], tiled=True)


def on_device(q_in, k_in, v_in, fir, skip, taps, segments, gain):
    width = q_in.shape[1]
    sources = (
        taps, k_in, v_in, q_in, fir, skip.reshape(1, width), gain.reshape(1, width),
        segments.reshape(1, TB),
    )
    payload, band, weight, rows, query = pl.pallas_call(
        prepare_kernel,
        out_shape=(
            pltpu.VMEM((NB, ROWS, TB), BF16),
            pltpu.VMEM((NB + 1, TB, TB), BF16),
            pltpu.VMEM((7, CH, TB), F32),
            pltpu.VMEM((8, width), F32),
            pltpu.VMEM((TB, width), BF16),
        ),
        in_specs=[pl.BlockSpec(memory_space=pl.ANY)] * 8,
        out_specs=(VM,) * 5,
        scratch_shapes=[pltpu.VMEM(value.shape, value.dtype) for value in sources if value is not q_in]
        + [pltpu.VMEM((GW, GW), F32), pltpu.SemaphoreType.DMA((8,))],
        name="prepare",
    )(*sources)
    payload = exchange(payload, "ctx", CTX_ORDER)
    mixed, gate = pl.pallas_call(
        conv_kernel,
        out_shape=(pltpu.VMEM((NB, CH, TB), BF16), pltpu.VMEM((width, TB), F32)),
        in_specs=[VM] * 5,
        out_specs=(VM,) * 2,
        name="conv",
    )(keep(payload), keep(band), keep(weight), keep(query), keep(rows))
    mixed = exchange(mixed, "ctx", CTX_ORDER)
    part, turned = pl.pallas_call(
        square_kernel,
        out_shape=(pltpu.VMEM((NB, 1, TB), F32), pltpu.VMEM((TB, width), F32)),
        in_specs=[VM] * 4,
        out_specs=(VM,) * 2,
        name="squares",
    )(keep(mixed), keep(gate), keep(payload), keep(rows))
    part = exchange(part, "grp", GRP_ORDER)
    return pl.pallas_call(
        finish_kernel,
        out_shape=jax.ShapeDtypeStruct((TB, width), BF16),
        in_specs=[VM] * 2,
        out_specs=VM,
        name="finish",
    )(keep(turned), keep(part))


def solution(mesh):
    return jax.shard_map(
        on_device,
        mesh=mesh,
        in_specs=(
            P("ctx", "grp"),
            P("ctx", "grp"),
            P("ctx", "grp"),
            P(None, None, "grp"),
            P("grp"),
            P("grp", None),
            P("ctx"),
            P("grp"),
        ),
        out_specs=P("ctx", "grp"),
        check_vma=False,
    )
```
